32 devices in a mesh: group: 2 (over y), section: 4 (over z), ctx: 2 (over core), head: 2 (over x).
Axes of the slice: x: 2, y: 2, z: 4, core: 2. Of those that a mesh axis runs over, the one named last changes fastest.
Arguments:
- queries: bfloat16 [2048, 48, 128], P(('group', 'section'), 'head'), parts along dimension 0, may hold values from -6 to 6
- slice_kv: bfloat16 [2048, 2, 128], P(('group', 'section')), parts along dimension 0, may hold values from -6 to 6
- cache_keys: bfloat16 [8, 16, 128, 128], P(('group', 'section'), 'ctx'), parts along dimension 0
- cache_values: bfloat16 [8, 16, 128, 128], P(('group', 'section'), 'ctx'), parts along dimension 0, may hold values from -6 to 6
- block_table: int32 [8, 16], P('group'), parts along dimension 0, may hold values from 0 to 15, each once within a row
- slice_index: int32 [8], P('group'), parts along dimension 0, may hold values from 0 to 3, as said below
- out_weight: bfloat16 [48, 128, 6144], P('head', 'section', 'ctx'), may hold values from -0.078125 to 0.078125
Outputs:
- mixed: bfloat16 [2048, 6144], P(('group', 'section'), ('ctx', 'head')), parts along dimension 0
The draws below stay inside these ranges and needn't reach their ends.
There are 2 independent parts, one for each index of `group`. The reference program is written for one: setup_inputs(seed, part) draws one part's arguments, and reference() takes and returns one part's arrays. A program takes and returns all parts, laid end to end along the dimension named above; an argument that names none is the same for every part. Nothing has to cross between parts.
Inputs may be any that keep to these rules, and one draw needn't show every extreme that they name: `slice_index`: every value appears once; the sections s and s + 4 / 2 (for s < 2) hold slice indices that sum to 3.
All inputs are finite; a program needn't handle non-finite values.
Results may differ from the reference program's by a relative error of at most 0.018.
Values may be sent and summed in bfloat16 or wider, within the bound.
No kernel may reach another device: no remote copies, remote signals or barrier semaphores. Data moves between devices by JAX's collectives and lax.ppermute only.
A program may use at most 64 MiB of HBM per device.

```python
import jax
import jax.numpy as jnp
from jax import lax

D = 6144
HEADS = 48
HD = 128
BLK = 128
BPS = 4
SECTIONS = 4
POOL = 16
TOKENS = 1024


def draw_cache_keys(key, part):
    full_shape = (SECTIONS, POOL, BLK, HD)
    key_base, key_pick = jax.random.split(jax.random.fold_in(key, 11), 2)
    picked = jax.random.bernoulli(key_pick, 1.0 / 32.0, (SECTIONS, POOL, BLK, 1))
    spread = jnp.where(picked, 3.0, 1.0).astype(jnp.float32)
    normal_part = jax.random.normal(key_base, full_shape, jnp.float32)
    return (spread * normal_part).astype(jnp.bfloat16)


def draw_slice_index(key, part):
    section_count = POOL // BPS
    half_count = section_count // 2
    key_perm, key_coin = jax.random.split(jax.random.fold_in(key, 23))
    values_perm = jax.random.permutation(key_perm, jnp.arange(half_count, dtype=jnp.int32))
    coin_flip = jax.random.randint(key_coin, (half_count,), 0, 2, dtype=jnp.int32)
    left_part = jnp.where(coin_flip == 1, values_perm, section_count - 1 - values_perm)
    right_part = section_count - 1 - left_part
    return jnp.concatenate([left_part, right_part]).astype(jnp.int32)


def block_scale(own_key, extent, pieces, low, high):
    gain = 1.0
    for axis_at, shards_of in pieces:
        steps = jax.random.uniform(jax.random.fold_in(jax.random.fold_in(own_key, 6), axis_at), (shards_of,), jnp.float32, low / len(pieces), high / len(pieces))
        gain = gain * jnp.repeat(jnp.exp(steps), extent[axis_at] // shards_of).reshape((-1,) + (1,) * (len(extent) - 1 - axis_at))
    return gain


def gaussian(stream_key, dims, width, bound, cuts=(), held_as=jnp.bfloat16):
    drawn = jax.random.normal(stream_key, dims, jnp.float32) * width
    if len(cuts) > 0:
        drawn = block_scale(stream_key, dims, cuts, -0.22, 0.18) * drawn
    return jnp.clip(drawn, min=-bound, max=bound).astype(held_as)


def setup_inputs(seed: int = 0, part: int = 0) -> dict:
    splits = jax.random.split(jax.random.key(seed), 8)
    own_keys = jax.random.split(jax.random.fold_in(splits[7], part), 8)
    return {
        "queries": gaussian(own_keys[0], (TOKENS, HEADS, HD), 1.0, 6.0, ((0, 4), (1, 2))),
        "slice_kv": gaussian(own_keys[1], (TOKENS, 2, HD), 1.0, 6.0, ((0, 4),)),
        "cache_keys": draw_cache_keys(jax.random.fold_in(jax.random.fold_in(splits[7], part), 71), part),
        "cache_values": gaussian(own_keys[3], (SECTIONS, POOL, BLK, HD), 1.0, 6.0, ((0, 4), (1, 2))),
        "block_table": jax.vmap(lambda own: jax.random.permutation(own, POOL))(jax.random.split(own_keys[4], SECTIONS)).reshape((SECTIONS, POOL)).astype(jnp.int32),
        "slice_index": draw_slice_index(jax.random.fold_in(jax.random.fold_in(splits[7], part), 71), part),
        "out_weight": gaussian(splits[6], (HEADS, HD, D), (HEADS * HD) ** -0.5, 0.078125, ((0, 2), (1, 4), (2, 2))),
    }


negative_floor = -1e30


def reference(queries, slice_kv, cache_keys, cache_values, block_table, slice_index, out_weight):
    section_count = block_table.shape[0]
    pool_size = block_table.shape[1]
    slice_len = queries.shape[0] // section_count
    head_count = queries.shape[1]
    head_dim = queries.shape[2]
    block_len = cache_keys.shape[2]
    score_scale = 1.0 / (head_dim ** 0.5)
    grouped_queries = queries.reshape(section_count, slice_len, head_count, head_dim)
    grouped_kv = slice_kv.reshape(section_count, slice_len, 2, head_dim)

    def one_section(section_items):
        section_queries, section_kv, section_keys, section_values, table_row, slice_number = section_items
        block_ids = jnp.arange(pool_size, dtype=jnp.int32)
        block_rank = jnp.sum(jnp.where(table_row[None, :] == block_ids[:, None], block_ids[None, :], 0), axis=1)
        active = block_rank < (slice_number + 1) * BPS
        cache_live = jnp.repeat(active, block_len)
        positions = jnp.arange(slice_len, dtype=jnp.int32)
        own_live = positions[None, :] <= positions[:, None]
        visible = jnp.concatenate([jnp.broadcast_to(cache_live[None, :], (slice_len, pool_size * block_len)), own_live], axis=1)
        all_keys = jnp.concatenate([section_keys.reshape(-1, head_dim), section_kv[:, 0]], axis=0).astype(jnp.float32)
        all_values = jnp.concatenate([section_values.reshape(-1, head_dim), section_kv[:, 1]], axis=0).astype(jnp.float32)

        def one_head(head_queries):
            scores = jnp.dot(head_queries.astype(jnp.float32), all_keys.T, precision=lax.Precision.HIGHEST) * score_scale
            masked = jnp.where(visible, scores, negative_floor)
            row_max = jnp.max(masked, axis=1)
            weights = jnp.where(visible, jnp.exp(masked - row_max[:, None]), 0.0)
            norm_sum = jnp.sum(weights, axis=1)
            numerator = jnp.dot(weights.astype(jnp.bfloat16).astype(jnp.float32), all_values, precision=lax.Precision.HIGHEST)
            return (numerator / norm_sum[:, None]).astype(jnp.bfloat16)

        per_head = lax.map(one_head, jnp.swapaxes(section_queries, 0, 1))
        return jnp.swapaxes(per_head, 0, 1)

    attended = lax.map(one_section, (grouped_queries, grouped_kv, cache_keys, cache_values, block_table, slice_index))
    flattened = attended.reshape(section_count * slice_len, head_count * head_dim).astype(jnp.float32)
    projection = out_weight.reshape(head_count * head_dim, -1).astype(jnp.float32)
    mixed = jnp.dot(flattened, projection, precision=lax.Precision.HIGHEST)
    return mixed.astype(jnp.bfloat16)
```

```python
import functools
import math

import jax
import jax.numpy as jnp
from jax import lax
from jax.experimental import pallas as pl
from jax.experimental.pallas import tpu as pltpu
from jax.sharding import PartitionSpec as P

BPS = 4

negative_floor = -1e30
column_chunks = 2


def attend_kernel(
    ids_ref, table_ref, index_ref, q_ref, own_ref, kl_ref, vl_ref, kr_ref, vr_ref, *rest, pieces
):
    out_refs = rest[:-4]
    k_s, v_s, m_s, acc_s = rest[-4:]
    heads, slice_len, head_dim = q_ref.shape
    local_pool, block_len = kl_ref.shape[:2]
    pool = table_ref.shape[1]
    section = ids_ref[0]
    ctx = ids_ref[1]
    steps = index_ref[section] + 1
    width = BPS * block_len
    factor = math.log2(math.e) / math.sqrt(head_dim)

    @pl.when(pl.program_id(0) == 0)
    def _():
        k_s[:slice_len, :] = own_ref[0]
        v_s[:slice_len, :head_dim] = own_ref[1]
        v_s[:, head_dim:] = jnp.ones((v_s.shape[0], v_s.shape[1] - head_dim), v_s.dtype)

        @pl.loop(0, steps * BPS)
        def _(j):
            place = lax.rem(table_ref[section, j] + pool - ctx * local_pool, pool)
            rows = pl.ds(pl.multiple_of(slice_len + j * block_len, block_len), block_len)

            @pl.when(place < local_pool)
            def _():
                k_s[rows, :] = kl_ref[place]
                v_s[rows, :head_dim] = vl_ref[place]

            @pl.when(place >= local_pool)
            def _():
                k_s[rows, :] = kr_ref[place - local_pool]
                v_s[rows, :head_dim] = vr_ref[place - local_pool]

    def scores(h, keys):
        return lax.dot_general(
            q_ref[h], keys, (((1,), (1,)), ((), ())), preferred_element_type=jnp.float32
        )

    own_keys = k_s[:slice_len, :]
    own_values = v_s[:slice_len, :]
    visible = lax.broadcasted_iota(jnp.int32, (slice_len, slice_len), 1) <= (
        lax.broadcasted_iota(jnp.int32, (slice_len, slice_len), 0)
    )
    for h in range(heads):
        s = jnp.where(visible, scores(h, own_keys), negative_floor)
        m = jnp.max(s, axis=1, keepdims=True)
        p = jnp.exp2(s * factor - m * factor).astype(jnp.bfloat16)
        m_s[h] = jnp.broadcast_to(m, m_s.shape[1:])
        acc_s[h] = jnp.dot(p, own_values, preferred_element_type=jnp.float32)

    @pl.loop(0, steps)
    def _(j):
        rows = pl.ds(pl.multiple_of(slice_len + j * width, block_len), width)
        keys = k_s[rows, :]
        values = v_s[rows, :]
        for h in range(heads):
            s = scores(h, keys)
            before = m_s[h][:, :1]
            m = jnp.maximum(before, jnp.max(s, axis=1, keepdims=True))
            p = jnp.exp2(s * factor - m * factor).astype(jnp.bfloat16)
            rescale = jnp.exp2((before - m) * factor)
            m_s[h] = jnp.broadcast_to(m, m_s.shape[1:])
            acc_s[h] = acc_s[h] * rescale + jnp.dot(p, values, preferred_element_type=jnp.float32)

    def attended(h):
        acc = acc_s[h]
        return acc[:, :head_dim] / acc[:, head_dim : 2 * head_dim]

    if pieces == 1:
        for h in range(heads):
            out_refs[0][h] = attended(h).astype(jnp.bfloat16)
    else:
        piece = head_dim // pieces
        lane_piece = lax.broadcasted_iota(jnp.int32, (slice_len, head_dim), 1) // piece
        turned = [
            attended(h) if h == 0 else pltpu.roll(attended(h), piece * h, 1) for h in range(heads)
        ]
        for k in range(pieces):
            which = lax.rem(section + k, pieces)
            picked = turned[0]
            for h in range(1, heads):
                picked = jnp.where(lane_piece == lax.rem(which + h, pieces), turned[h], picked)
            picked = pltpu.roll(picked, head_dim - piece * which, 1)
            out_refs[k][...] = picked.astype(jnp.bfloat16)


def attend(ids, block_table, slice_index, q, own, kl, vl, kr, vr, group, pieces):
    heads, slice_len, head_dim = q.shape
    local_pool, block_len = kl.shape[:2]
    pool = block_table.shape[1]
    rows = slice_len + pool * block_len
    groups = heads // group
    whole = lambda a: pl.BlockSpec(a.shape, lambda g, *_: (0,) * a.ndim)
    if pieces == 1:
        out_shape = [jax.ShapeDtypeStruct(q.shape, jnp.bfloat16)]
        out_specs = [pl.BlockSpec((group, slice_len, head_dim), lambda g, *_: (g, 0, 0))]
    else:
        out_shape = [jax.ShapeDtypeStruct((slice_len, groups * head_dim), jnp.bfloat16)] * pieces
        out_specs = [pl.BlockSpec((slice_len, head_dim), lambda g, *_: (0, g))] * pieces
    return pl.pallas_call(
        functools.partial(attend_kernel, pieces=pieces),
        out_shape=out_shape,
        grid_spec=pltpu.PrefetchScalarGridSpec(
            num_scalar_prefetch=3,
            grid=(groups,),
            in_specs=[
                pl.BlockSpec((group, slice_len, head_dim), lambda g, *_: (g, 0, 0)),
                whole(own),
                whole(kl),
                whole(vl),
                whole(kr),
                whole(vr),
            ],
            out_specs=out_specs,
            scratch_shapes=[
                pltpu.VMEM((rows, head_dim), jnp.bfloat16),
                pltpu.VMEM((rows, 2 * head_dim), jnp.bfloat16),
                pltpu.VMEM((group, slice_len, 128), jnp.float32),
                pltpu.VMEM((group, slice_len, 2 * head_dim), jnp.float32),
            ],
        ),
        compiler_params=pltpu.CompilerParams(dimension_semantics=("arbitrary",)),
        name="attend",
    )(ids, block_table, slice_index, q, own, kl, vl, kr, vr)


def project_kernel(ids_ref, *refs, sections):
    a_refs = refs[: 4 * sections]
    w_refs = refs[4 * sections : 4 * sections + 4]
    out_refs = refs[4 * sections + 4 : 5 * sections + 4]
    a_s, w_s = refs[5 * sections + 4 :]
    slice_len, part = a_refs[0].shape
    straight = ids_ref[1] == ids_ref[3]

    @pl.when(pl.program_id(0) == 0)
    def _():
        for k in range(sections):
            own, other, across, across_other = a_refs[4 * k : 4 * k + 4]
            rows = slice(k * slice_len, (k + 1) * slice_len)
            a_s[rows, :part] = own[...]
            a_s[rows, part : 2 * part] = other[...]

            @pl.when(straight)
            def _():
                a_s[rows, 2 * part : 3 * part] = across[...]
                a_s[rows, 3 * part :] = across_other[...]

            @pl.when(jnp.logical_not(straight))
            def _():
                a_s[rows, 2 * part : 3 * part] = across_other[...]
                a_s[rows, 3 * part :] = across[...]

    for i in range(4):
        w_s[i * part : (i + 1) * part, :] = w_refs[i][...]
    weights = w_s[...]
    for k in range(sections):
        out_refs[k][...] = jnp.dot(
            a_s[k * slice_len : (k + 1) * slice_len, :],
            weights,
            preferred_element_type=jnp.float32,
        ).astype(jnp.bfloat16)


def project(ids, pieces, w_local, w_first, w_second, chunk, columns):
    sections = len(pieces)
    slice_len, part = pieces[0][0].shape
    tile = math.gcd(columns, 256)
    per_chunk = columns // tile
    per_half = w_first.shape[1] // tile
    base = chunk * per_chunk
    flat = [a for four in pieces for a in four]
    return pl.pallas_call(
        functools.partial(project_kernel, sections=sections),
        out_shape=[jax.ShapeDtypeStruct((slice_len, columns), jnp.bfloat16)] * sections,
        grid_spec=pltpu.PrefetchScalarGridSpec(
            num_scalar_prefetch=1,
            grid=(per_chunk,),
            in_specs=[pl.BlockSpec(a.shape, lambda n, ids: (0, 0)) for a in flat]
            + [
                pl.BlockSpec((part, tile), lambda n, ids: (ids[1], ids[2] * per_half + base + n)),
                pl.BlockSpec(
                    (part, tile), lambda n, ids: (1 - ids[1], ids[2] * per_half + base + n)
                ),
                pl.BlockSpec((part, tile), lambda n, ids: (0, base + n)),
                pl.BlockSpec((part, tile), lambda n, ids: (0, base + n)),
            ],
            out_specs=[pl.BlockSpec((slice_len, tile), lambda n, ids: (0, n))] * sections,
            scratch_shapes=[
                pltpu.VMEM((sections * slice_len, 4 * part), jnp.bfloat16),
                pltpu.VMEM((4 * part, tile), jnp.bfloat16),
            ],
        ),
        compiler_params=pltpu.CompilerParams(dimension_semantics=("arbitrary",)),
        name="project",
    )(ids, *flat, w_local, w_local, w_first, w_second)


swap = [(0, 1), (1, 0)]


def add_rounded(*values):
    total = values[0].astype(jnp.float32)
    for value in values[1:]:
        total = total + value.astype(jnp.float32)
    return total.astype(jnp.bfloat16)


def line_reduce(partial):
    count = len(partial)
    up = down = None
    for t in range(1, count):
        send_up = partial[t] if up is None else add_rounded(partial[t], up)
        send_down = partial[count - t] if down is None else add_rounded(partial[count - t], down)
        up = lax.ppermute(send_up, "section", [(z, z + 1) for z in range(t)])
        down = lax.ppermute(
            send_down, "section", [(count - 1 - z, count - 2 - z) for z in range(t)]
        )
    return add_rounded(partial[0], up, down)


def on_device(queries, slice_kv, cache_keys, cache_values, block_table, slice_index, out_weight):
    slice_len, heads_here, head_dim = queries.shape
    section_count = lax.axis_size("section")
    ctx_count = lax.axis_size("ctx")
    head_count = lax.axis_size("head")
    group_count = lax.axis_size("group")
    section = lax.axis_index("section")
    ctx = lax.axis_index("ctx")
    head = lax.axis_index("head")
    group = lax.axis_index("group")
    ids = jnp.stack([section, ctx, head, group]).astype(jnp.int32)
    core_heads = heads_here // ctx_count
    pairs = (
        ctx_count == 2
        and head_count == 2
        and group_count == 2
        and head_dim % section_count == 0
        and core_heads % section_count == 0
        and (core_heads * head_dim // section_count) % 128 == 0
    )
    width = out_weight.shape[2]
    w_local = out_weight.reshape(heads_here * out_weight.shape[1], width)
    out_columns = width // head_count

    keys_far = lax.ppermute(cache_keys[0], "ctx", swap)
    values_far = lax.ppermute(cache_values[0], "ctx", swap)
    if pairs:
        half_rows = w_local.shape[0] // 2
        sent = lax.dynamic_slice(
            w_local,
            (group * half_rows, (1 - head) * out_columns),
            (half_rows, out_columns),
        )
        w_first = lax.ppermute(sent, "head", swap)
        w_second = lax.ppermute(w_first, "group", swap)
    own_queries = lax.dynamic_slice_in_dim(queries, ctx * core_heads, core_heads, 1)
    q = jnp.swapaxes(own_queries, 0, 1)
    own = jnp.swapaxes(slice_kv, 0, 1)
    if pairs:
        sent_parts = attend(
            ids, block_table, slice_index, q, own, cache_keys[0], cache_values[0],
            keys_far, values_far, section_count, section_count,
        )
        mine = [sent_parts[0]] + [None] * (section_count - 1)
        for k in range(1, section_count):
            mine[k] = lax.ppermute(
                sent_parts[k],
                "section",
                [(z, (z + k) % section_count) for z in range(section_count)],
            )
        pieces = []
        for k in range(section_count):
            across = lax.ppermute(mine[k], "head", swap)
            pieces.append(
                (
                    mine[k],
                    lax.ppermute(mine[k], "ctx", swap),
                    across,
                    lax.ppermute(across, "ctx", swap),
                )
            )
        columns = out_columns // column_chunks
        reduced = []
        for chunk in range(column_chunks):
            partial = project(ids, pieces, w_local, w_first, w_second, chunk, columns)
            reduced.append(line_reduce(partial))
        return jnp.concatenate(reduced, axis=1)

    heads_at_once = math.gcd(core_heads, 4) if core_heads % 3 else 3
    attended = attend(
        ids, block_table, slice_index, q, own, cache_keys[0], cache_values[0],
        keys_far, values_far, heads_at_once, 1,
    )[0]
    piece = head_dim // section_count
    by_section = attended.reshape(core_heads, slice_len, section_count, piece)
    by_section = by_section.transpose(2, 1, 0, 3).reshape(section_count, slice_len, -1)
    gathered = lax.all_to_all(by_section, "section", 0, 0)
    rows = gathered.reshape(section_count * slice_len, core_heads * piece)
    rows = lax.all_gather(rows, ("head", "ctx"), axis=1, tiled=True)
    weights = lax.all_to_all(w_local, "head", split_axis=1, concat_axis=0, tiled=True)
    partial = jnp.dot(rows, weights, preferred_element_type=jnp.float32).astype(jnp.bfloat16)
    return lax.psum_scatter(partial, "section", scatter_dimension=0, tiled=True)


def solution(mesh):
    placed = (
        P(("group", "section"), "head", None),
        P(("group", "section"), None, None),
        P(("group", "section"), "ctx", None, None),
        P(("group", "section"), "ctx", None, None),
        P("group", None),
        P("group"),
        P("head", "section", "ctx"),
    )
    return jax.shard_map(
        on_device,
        mesh=mesh,
        in_specs=placed,
        out_specs=P(("group", "section"), ("ctx", "head")),
        check_vma=False,
    )
```

```python
import functools
import math

import jax
import jax.numpy as jnp
from jax import lax
from jax.experimental import pallas as pl
from jax.experimental.pallas import tpu as pltpu
from jax.sharding import PartitionSpec as P


BPS = 4

negative_floor = -1e30
column_chunks = 2


def attend_kernel(ids_ref, table_ref, index_ref, q_ref, *refs, first, pieces, block_len):
    if first:
        own_ref, kl_ref, vl_ref, kr_ref, vr_ref = refs[:5]
        out_refs = refs[5:-4]
        k_s, vt_s, m_s, acc_s = refs[-4:]
    else:
        k_s, vt_s = refs[:2]
        out_refs = refs[2:-2]
        m_s, acc_s = refs[-2:]
    heads, tokens, head_dim = q_ref.shape
    pool = table_ref.shape[1]
    section = ids_ref[0]
    ctx = ids_ref[1]
    slice_len = k_s.shape[0] - pool * block_len
    steps = index_ref[section] + 1
    width = BPS * block_len
    factor = math.log2(math.e) / math.sqrt(head_dim)

    if first:
        local_pool = kl_ref.shape[0]
        k_s[:slice_len, :] = own_ref[0]
        vt_s[:head_dim, :slice_len] = own_ref[1].T
        vt_s[head_dim:, :] = jnp.ones((vt_s.shape[0] - head_dim, vt_s.shape[1]), vt_s.dtype)

        @pl.loop(0, steps * BPS)
        def _(j):
            place = lax.rem(table_ref[section, j] + pool - ctx * local_pool, pool)
            rows = pl.ds(pl.multiple_of(slice_len + j * block_len, block_len), block_len)

            @pl.when(place < local_pool)
            def _():
                k_s[rows, :] = kl_ref[place]
                vt_s[:head_dim, rows] = vl_ref[place].T

            @pl.when(place >= local_pool)
            def _():
                k_s[rows, :] = kr_ref[place - local_pool]
                vt_s[:head_dim, rows] = vr_ref[place - local_pool].T

    q = q_ref[...].reshape(heads * tokens, head_dim)

    def scores(keys):
        return lax.dot_general(
            keys, q, (((1,), (1,)), ((), ())), preferred_element_type=jnp.float32
        )

    shape = (slice_len, heads * tokens)
    token = lax.rem(lax.broadcasted_iota(jnp.int32, shape, 1), tokens) + ctx * tokens
    s = jnp.where(
        lax.broadcasted_iota(jnp.int32, shape, 0) <= token, scores(k_s[:slice_len, :]), negative_floor
    )
    m = jnp.max(s, axis=0, keepdims=True)
    p = jnp.exp2(s * factor - m * factor).astype(jnp.bfloat16)
    m_s[...] = jnp.broadcast_to(m, m_s.shape)
    acc_s[...] = jnp.dot(vt_s[:, :slice_len], p, preferred_element_type=jnp.float32)

    @pl.loop(0, steps)
    def _(j):
        rows = pl.ds(pl.multiple_of(slice_len + j * width, block_len), width)
        s = scores(k_s[rows, :])
        before = m_s[:1, :]
        m = jnp.maximum(before, jnp.max(s, axis=0, keepdims=True))
        p = jnp.exp2(s * factor - m * factor).astype(jnp.bfloat16)
        rescale = jnp.exp2((before - m) * factor)
        m_s[...] = jnp.broadcast_to(m, m_s.shape)
        acc_s[...] = acc_s[...] * rescale + jnp.dot(
            vt_s[:, rows], p, preferred_element_type=jnp.float32
        )

    acc_s[:head_dim, :] = acc_s[:head_dim, :] / acc_s[head_dim : head_dim + 1, :]
    if pieces == 1:
        out_refs[0][...] = acc_s[:head_dim, :].astype(jnp.bfloat16)
    else:
        piece = head_dim // pieces
        for k in range(pieces):
            rows = pl.ds(pl.multiple_of(lax.rem(section + k, pieces) * piece, piece), piece)
            for h in range(heads):
                out_refs[k][h * piece : (h + 1) * piece, :] = acc_s[
                    rows, h * tokens : (h + 1) * tokens
                ].astype(jnp.bfloat16)


def attend(ids, block_table, slice_index, q, arrays, block_len, first_head, heads, pieces, first):
    tokens, head_dim = q.shape[1:]
    whole = lambda a: pl.BlockSpec(a.shape, lambda g, *_: (0,) * a.ndim)
    pool = block_table.shape[1]
    if first:
        keys = arrays[0].shape[1] + pool * arrays[1].shape[1]
        packed = [
            jax.ShapeDtypeStruct((keys, head_dim), jnp.bfloat16),
            jax.ShapeDtypeStruct((head_dim + 16, keys), jnp.bfloat16),
        ]
    else:
        packed = []
    if pieces == 1:
        out_shape = [jax.ShapeDtypeStruct((head_dim, heads * tokens), jnp.bfloat16)]
    else:
        out_shape = [
            jax.ShapeDtypeStruct((heads * head_dim // pieces, tokens), jnp.bfloat16)
        ] * pieces
    block = first_head // heads
    outs = pl.pallas_call(
        functools.partial(attend_kernel, first=first, pieces=pieces, block_len=block_len),
        out_shape=out_shape + packed,
        grid_spec=pltpu.PrefetchScalarGridSpec(
            num_scalar_prefetch=3,
            grid=(1,),
            in_specs=[pl.BlockSpec((heads, tokens, head_dim), lambda g, *_: (block, 0, 0))]
            + [whole(a) for a in arrays],
            out_specs=[whole(a) for a in out_shape + packed],
            scratch_shapes=[
                pltpu.VMEM((8, heads * tokens), jnp.float32),
                pltpu.VMEM((head_dim + 16, heads * tokens), jnp.float32),
            ],
        ),
        compiler_params=pltpu.CompilerParams(dimension_semantics=("arbitrary",)),
        name="attend",
    )(ids, block_table, slice_index, q, *arrays)
    return list(outs[: len(out_shape)]), list(outs[len(out_shape) :])


def project_kernel(ids_ref, *refs, sections, parts):
    near = refs[: sections * parts]
    far = refs[sections * parts : 2 * sections * parts]
    w_refs = refs[2 * sections * parts : 2 * sections * parts + 6]
    out_refs = refs[2 * sections * parts + 6 : -1]
    a_s = refs[-1]
    rows, tokens = near[0].shape
    all_rows = rows * parts
    half = all_rows // 2
    group = ids_ref[3]

    @pl.when(pl.program_id(0) == 0)
    def _():
        for k in range(sections):
            at = slice(k * tokens, (k + 1) * tokens)
            for i in range(parts):
                a_s[at, i * rows : (i + 1) * rows] = near[k * parts + i][...].T
                place = all_rows + lax.rem(i + group, parts) * rows
                a_s[at, pl.ds(pl.multiple_of(place, rows), rows)] = far[k * parts + i][...].T

    a = a_s[...]
    for side in range(2):
        own, one, two = w_refs[3 * side : 3 * side + 3]
        out = jnp.dot(a[:, :all_rows], own[...], preferred_element_type=jnp.float32)
        out = out + jnp.dot(
            a[:, all_rows : all_rows + half], one[...], preferred_element_type=jnp.float32
        )
        out = out + jnp.dot(
            a[:, all_rows + half :], two[...], preferred_element_type=jnp.float32
        )
        for k in range(sections):
            out_refs[k][side] = out[k * tokens : (k + 1) * tokens].astype(jnp.bfloat16)


def project(ids, near, far, weights, chunk, columns):
    sections, parts = len(near), len(near[0])
    rows, tokens = near[0][0].shape
    tile = math.gcd(columns, 256)
    per_chunk = columns // tile
    per_half = weights[3].shape[1] // tile
    base = chunk * per_chunk
    flat = [a for both in (near, far) for k in both for a in k]
    here = lambda n, ids: (0, base + n)
    start = lambda n, ids: (0, n)
    return pl.pallas_call(
        functools.partial(project_kernel, sections=sections, parts=parts),
        out_shape=[jax.ShapeDtypeStruct((2, tokens, columns), jnp.bfloat16)] * sections,
        grid_spec=pltpu.PrefetchScalarGridSpec(
            num_scalar_prefetch=1,
            grid=(per_chunk,),
            in_specs=[pl.BlockSpec(a.shape, lambda n, ids: (0, 0)) for a in flat]
            + [
                pl.BlockSpec(
                    (weights[0].shape[0], tile), lambda n, ids: (0, ids[2] * per_half + base + n)
                )
            ]
            + [
                pl.BlockSpec((w.shape[0], tile), here if w is weights[3] else start)
                for w in weights[1:]
            ],
            out_specs=[pl.BlockSpec((2, tokens, tile), lambda n, ids: (0, 0, n))] * sections,
            scratch_shapes=[pltpu.VMEM((sections * tokens, 2 * parts * rows), jnp.bfloat16)],
        ),
        compiler_params=pltpu.CompilerParams(dimension_semantics=("arbitrary",)),
        name="project",
    )(ids, *flat, *weights)


def combine_kernel(ids_ref, own, up, down, twin, cross_up, cross_down, *rest):
    out = rest[-1]
    tokens = own.shape[0]
    f32 = lambda ref: ref[...].astype(jnp.float32)
    ctx = ids_ref[1]
    here = pl.ds(pl.multiple_of(ctx * tokens, tokens), tokens)
    there = pl.ds(pl.multiple_of((1 - ctx) * tokens, tokens), tokens)
    out[here, :] = (f32(own) + f32(up) + f32(down)).astype(jnp.bfloat16)
    out[there, :] = (f32(twin) + f32(cross_up) + f32(cross_down)).astype(jnp.bfloat16)


def combine(ids, own, up, down, twin, cross_up, cross_down, before, chunk, chunks):
    tokens, columns = twin.shape
    flat = [own, up, down, twin, cross_up, cross_down]
    specs = [
        pl.BlockSpec((None, tokens, columns), lambda g, ids: (0, 0, 0))
        if a.ndim == 3
        else pl.BlockSpec((tokens, columns), lambda g, ids: (0, 0))
        for a in flat
    ]
    args = flat
    aliases = {}
    if before is not None:
        specs = specs + [pl.BlockSpec(memory_space=pl.ANY)]
        args = flat + [before]
        aliases = {7: 0}
    return pl.pallas_call(
        combine_kernel,
        out_shape=jax.ShapeDtypeStruct((2 * tokens, columns * chunks), jnp.bfloat16),
        grid_spec=pltpu.PrefetchScalarGridSpec(
            num_scalar_prefetch=1,
            grid=(1,),
            in_specs=specs,
            out_specs=pl.BlockSpec((2 * tokens, columns), lambda g, ids: (0, chunk)),
        ),
        input_output_aliases=aliases,
        name="combine",
    )(ids, *args)


swap = [(0, 1), (1, 0)]


def add_rounded(*values):
    total = values[0].astype(jnp.float32)
    for value in values[1:]:
        total = total + value.astype(jnp.float32)
    return total.astype(jnp.bfloat16)


def line_reduce(partial):
    count = len(partial)
    up = down = None
    for t in range(1, count):
        send_up = partial[t] if up is None else add_rounded(partial[t], up)
        send_down = partial[count - t] if down is None else add_rounded(partial[count - t], down)
        ups = [(z, z + 1) for z in range(t)]
        downs = [(count - 1 - z, count - 2 - z) for z in range(t)]
        if t + 1 < count:
            up = lax.ppermute(send_up, "section", ups)
            down = lax.ppermute(send_down, "section", downs)
    crossed = lambda pairs: [(2 * i + c, 2 * j + 1 - c) for i, j in pairs for c in range(2)]
    twin = lax.ppermute(partial[0][1], "ctx", swap)
    return (
        partial[0],
        lax.ppermute(send_up[0], "section", ups),
        lax.ppermute(send_down[0], "section", downs),
        twin,
        lax.ppermute(send_up[1], ("section", "ctx"), crossed(ups)),
        lax.ppermute(send_down[1], ("section", "ctx"), crossed(downs)),
    )


def on_device(queries, slice_kv, cache_keys, cache_values, block_table, slice_index, out_weight):
    slice_len, heads, head_dim = queries.shape
    section_count = lax.axis_size("section")
    ctx_count = lax.axis_size("ctx")
    head_count = lax.axis_size("head")
    group_count = lax.axis_size("group")
    section = lax.axis_index("section")
    ctx = lax.axis_index("ctx")
    head = lax.axis_index("head")
    group = lax.axis_index("group")
    ids = jnp.stack([section, ctx, head, group]).astype(jnp.int32)
    tokens = slice_len // ctx_count
    block_len = cache_keys.shape[2]
    piece = head_dim // section_count
    width = out_weight.shape[2]
    w_local = out_weight.reshape(heads * piece, width)
    out_columns = width // head_count
    pairs = (
        head_count == 2
        and group_count == 2
        and piece % 16 == 0
        and heads % 2 == 0
        and out_columns % (128 * column_chunks) == 0
    )

    keys_far = lax.ppermute(cache_keys[0], "ctx", swap)
    values_far = lax.ppermute(cache_values[0], "ctx", swap)
    own_queries = lax.dynamic_slice_in_dim(queries, ctx * tokens, tokens, 0)
    q = jnp.swapaxes(own_queries, 0, 1)
    own = jnp.swapaxes(slice_kv, 0, 1)
    blocks = [own, cache_keys[0], cache_values[0], keys_far, values_far]
    if pairs:
        parts = 2
        columns = out_columns // column_chunks
        half_rows = w_local.shape[0] // 2
        w_one, w_two, twin_kept, twin_one, twin_two = ([None] * column_chunks for _ in range(5))
        for chunk in range(column_chunks):
            sent = lax.dynamic_slice(
                w_local,
                (group * half_rows, (1 - head) * out_columns + chunk * columns),
                (half_rows, columns),
            )
            w_one[chunk] = lax.ppermute(sent, "head", swap)
        w_kept = lax.dynamic_slice_in_dim(w_local, head * out_columns, out_columns, 1)
        twin_kept = lax.ppermute(w_kept, "ctx", swap)
        near = [[None] * parts for _ in range(section_count)]
        far = [[None] * parts for _ in range(section_count)]
        arrays = blocks
        for i in range(parts):
            made, packed = attend(
                ids, block_table, slice_index, q, arrays, block_len, i * (heads // parts),
                heads // parts, section_count, i == 0,
            )
            if i == 0:
                arrays = packed
            near[0][i] = made[0]
            for k in shift_order(section_count):
                near[k][i] = lax.ppermute(
                    made[k],
                    "section",
                    [(z, (z + k) % section_count) for z in range(section_count)],
                )
            for k in range(section_count):
                far[k][i] = lax.ppermute(near[k][i], "head", swap)
        for chunk in range(column_chunks):
            w_two[chunk] = lax.ppermute(w_one[chunk], "group", swap)
            twin_one[chunk] = lax.ppermute(w_one[chunk], "ctx", swap)
            twin_two[chunk] = lax.ppermute(w_two[chunk], "ctx", swap)
        out = None
        for chunk in range(column_chunks):
            weights = [w_local, w_one[chunk], w_two[chunk], twin_kept, twin_one[chunk], twin_two[chunk]]
            partial = project(ids, near, far, weights, chunk, columns)
            out = combine(ids, *line_reduce(partial), out, chunk, column_chunks)
        return out

    attended = attend(ids, block_table, slice_index, q, blocks, block_len, 0, heads, 1, True)[0][0]
    by_section = attended.reshape(section_count, piece, heads, tokens).transpose(0, 3, 2, 1)
    by_section = by_section.reshape(section_count, tokens, heads * piece)
    by_section = lax.all_gather(by_section, "ctx", axis=1, tiled=True)
    rows = lax.all_to_all(by_section, "section", 0, 0)
    rows = rows.reshape(section_count * slice_len, heads * piece)
    rows = lax.all_gather(rows, "head", axis=1, tiled=True)
    weights = lax.all_to_all(w_local, "head", split_axis=1, concat_axis=0, tiled=True)
    partial = jnp.dot(rows, weights, preferred_element_type=jnp.float32).astype(jnp.bfloat16)
    return lax.psum_scatter(partial, "section", scatter_dimension=0, tiled=True)


def shift_order(sections):
    return sorted(range(1, sections), key=lambda k: min(k, sections - k))


def solution(mesh):
    placed = (
        P(("group", "section"), "head", None),
        P(("group", "section"), None, None),
        P(("group", "section"), "ctx", None, None),
        P(("group", "section"), "ctx", None, None),
        P("group", None),
        P("group"),
        P("head", "section", "ctx"),
    )

    return jax.shard_map(
        on_device,
        mesh=mesh,
        in_specs=placed,
        out_specs=P(("group", "section"), ("ctx", "head")),
        check_vma=False,
    )
```

```python
import functools
import math

import jax
import jax.numpy as jnp
from jax import lax
from jax.experimental import pallas as pl
from jax.experimental.pallas import tpu as pltpu
from jax.sharding import PartitionSpec as P


BPS = 4

negative_floor = -1e30
column_chunks = 2


def attend_kernel(ids_ref, table_ref, index_ref, q_ref, *refs, first, pieces, block_len):
    if first:
        own_ref, kl_ref, vl_ref, kr_ref, vr_ref = refs[:5]
        out_refs = refs[5:-4]
        k_s, vt_s, m_s, acc_s = refs[-4:]
    else:
        k_s, vt_s = refs[:2]
        out_refs = refs[2:-2]
        m_s, acc_s = refs[-2:]
    heads, tokens, head_dim = q_ref.shape
    pool = table_ref.shape[1]
    section = ids_ref[0]
    ctx = ids_ref[1]
    slice_len = k_s.shape[0] - pool * block_len
    steps = index_ref[section] + 1
    width = BPS * block_len
    factor = math.log2(math.e) / math.sqrt(head_dim)

    if first:
        local_pool = kl_ref.shape[0]
        k_s[:slice_len, :] = own_ref[0]
        vt_s[:head_dim, :slice_len] = own_ref[1].T
        vt_s[head_dim:, :] = jnp.ones((vt_s.shape[0] - head_dim, vt_s.shape[1]), vt_s.dtype)

        @pl.loop(0, steps * BPS)
        def _(j):
            place = lax.rem(table_ref[section, j] + pool - ctx * local_pool, pool)
            rows = pl.ds(pl.multiple_of(slice_len + j * block_len, block_len), block_len)

            @pl.when(place < local_pool)
            def _():
                k_s[rows, :] = kl_ref[place]
                vt_s[:head_dim, rows] = vl_ref[place].T

            @pl.when(place >= local_pool)
            def _():
                k_s[rows, :] = kr_ref[place - local_pool]
                vt_s[:head_dim, rows] = vr_ref[place - local_pool].T

    q = q_ref[...].reshape(heads * tokens, head_dim)

    def scores(keys):
        return lax.dot_general(
            keys, q, (((1,), (1,)), ((), ())), preferred_element_type=jnp.float32
        )

    shape = (slice_len, heads * tokens)
    token = lax.rem(lax.broadcasted_iota(jnp.int32, shape, 1), tokens) + ctx * tokens
    s = jnp.where(
        lax.broadcasted_iota(jnp.int32, shape, 0) <= token, scores(k_s[:slice_len, :]), negative_floor
    )
    m = jnp.max(s, axis=0, keepdims=True)
    p = jnp.exp2(s * factor - m * factor).astype(jnp.bfloat16)
    m_s[...] = jnp.broadcast_to(m, m_s.shape)
    acc_s[...] = jnp.dot(vt_s[:, :slice_len], p, preferred_element_type=jnp.float32)

    @pl.loop(0, steps)
    def _(j):
        rows = pl.ds(pl.multiple_of(slice_len + j * width, block_len), width)
        s = scores(k_s[rows, :])
        before = m_s[:1, :]
        m = jnp.maximum(before, jnp.max(s, axis=0, keepdims=True))
        p = jnp.exp2(s * factor - m * factor).astype(jnp.bfloat16)
        rescale = jnp.exp2((before - m) * factor)
        m_s[...] = jnp.broadcast_to(m, m_s.shape)
        acc_s[...] = acc_s[...] * rescale + jnp.dot(
            vt_s[:, rows], p, preferred_element_type=jnp.float32
        )

    acc_s[:head_dim, :] = acc_s[:head_dim, :] / acc_s[head_dim : head_dim + 1, :]
    if pieces == 1:
        out_refs[0][...] = acc_s[:head_dim, :].astype(jnp.bfloat16)
    else:
        piece = head_dim // pieces
        for k in range(pieces):
            rows = pl.ds(pl.multiple_of(lax.rem(section + k, pieces) * piece, piece), piece)
            for h in range(heads):
                out_refs[k][h * piece : (h + 1) * piece, :] = acc_s[
                    rows, h * tokens : (h + 1) * tokens
                ].astype(jnp.bfloat16)


def attend(ids, block_table, slice_index, q, arrays, block_len, first_head, heads, pieces, first):
    tokens, head_dim = q.shape[1:]
    whole = lambda a: pl.BlockSpec(a.shape, lambda g, *_: (0,) * a.ndim)
    pool = block_table.shape[1]
    if first:
        keys = arrays[0].shape[1] + pool * arrays[1].shape[1]
        packed = [
            jax.ShapeDtypeStruct((keys, head_dim), jnp.bfloat16),
            jax.ShapeDtypeStruct((head_dim + 16, keys), jnp.bfloat16),
        ]
    else:
        packed = []
    if pieces == 1:
        out_shape = [jax.ShapeDtypeStruct((head_dim, heads * tokens), jnp.bfloat16)]
    else:
        out_shape = [
            jax.ShapeDtypeStruct((heads * head_dim // pieces, tokens), jnp.bfloat16)
        ] * pieces
    block = first_head // heads
    outs = pl.pallas_call(
        functools.partial(attend_kernel, first=first, pieces=pieces, block_len=block_len),
        out_shape=out_shape + packed,
        grid_spec=pltpu.PrefetchScalarGridSpec(
            num_scalar_prefetch=3,
            grid=(1,),
            in_specs=[pl.BlockSpec((heads, tokens, head_dim), lambda g, *_: (block, 0, 0))]
            + [whole(a) for a in arrays],
            out_specs=[whole(a) for a in out_shape + packed],
            scratch_shapes=[
                pltpu.VMEM((8, heads * tokens), jnp.float32),
                pltpu.VMEM((head_dim + 16, heads * tokens), jnp.float32),
            ],
        ),
        compiler_params=pltpu.CompilerParams(dimension_semantics=("arbitrary",)),
        name="attend",
    )(ids, block_table, slice_index, q, *arrays)
    return list(outs[: len(out_shape)]), list(outs[len(out_shape) :])


def project_kernel(ids_ref, *refs, sections, parts):
    near = refs[: sections * parts]
    far = refs[sections * parts : 2 * sections * parts]
    w_refs = refs[2 * sections * parts : 2 * sections * parts + 6]
    out_refs = refs[2 * sections * parts + 6 : -1]
    a_s = refs[-1]
    rows, tokens = near[0].shape
    all_rows = rows * parts
    half = all_rows // 2
    group = ids_ref[3]

    @pl.when(pl.program_id(0) == 0)
    def _():
        for k in range(sections):
            at = slice(k * tokens, (k + 1) * tokens)
            for i in range(parts):
                a_s[at, i * rows : (i + 1) * rows] = near[k * parts + i][...].T
                place = all_rows + lax.rem(i + group, parts) * rows
                a_s[at, pl.ds(pl.multiple_of(place, rows), rows)] = far[k * parts + i][...].T

    a = a_s[...]
    for side in range(2):
        own, one, two = w_refs[3 * side : 3 * side + 3]
        out = jnp.dot(a[:, :all_rows], own[...], preferred_element_type=jnp.float32)
        out = out + jnp.dot(
            a[:, all_rows : all_rows + half], one[...], preferred_element_type=jnp.float32
        )
        out = out + jnp.dot(
            a[:, all_rows + half :], two[...], preferred_element_type=jnp.float32
        )
        for k in range(sections):
            out_refs[k][side] = out[k * tokens : (k + 1) * tokens].astype(jnp.bfloat16)


def project(ids, near, far, weights, chunk, columns):
    sections, parts = len(near), len(near[0])
    rows, tokens = near[0][0].shape
    tile = math.gcd(columns, 256)
    per_chunk = columns // tile
    per_half = weights[0].shape[1] // 2 // tile
    base = chunk * per_chunk
    flat = [a for both in (near, far) for k in both for a in k]
    local = lambda n, ids: (0, ids[2] * per_half + base + n)
    sent = lambda n, ids: (0, n)
    return pl.pallas_call(
        functools.partial(project_kernel, sections=sections, parts=parts),
        out_shape=[jax.ShapeDtypeStruct((2, tokens, columns), jnp.bfloat16)] * sections,
        grid_spec=pltpu.PrefetchScalarGridSpec(
            num_scalar_prefetch=1,
            grid=(per_chunk,),
            in_specs=[pl.BlockSpec(a.shape, lambda n, ids: (0, 0)) for a in flat]
            + [
                pl.BlockSpec((w.shape[0], tile), sent if i % 3 else local)
                for i, w in enumerate(weights)
            ],
            out_specs=[pl.BlockSpec((2, tokens, tile), lambda n, ids: (0, 0, n))] * sections,
            scratch_shapes=[pltpu.VMEM((sections * tokens, 2 * parts * rows), jnp.bfloat16)],
        ),
        compiler_params=pltpu.CompilerParams(dimension_semantics=("arbitrary",)),
        name="project",
    )(ids, *flat, *weights)


def combine_kernel(ids_ref, own, up, down, twin, cross_up, cross_down, *rest):
    out = rest[-1]
    tokens = own.shape[0]
    f32 = lambda ref: ref[...].astype(jnp.float32)
    ctx = ids_ref[1]
    here = pl.ds(pl.multiple_of(ctx * tokens, tokens), tokens)
    there = pl.ds(pl.multiple_of((1 - ctx) * tokens, tokens), tokens)
    out[here, :] = (f32(own) + f32(up) + f32(down)).astype(jnp.bfloat16)
    out[there, :] = (f32(twin) + f32(cross_up) + f32(cross_down)).astype(jnp.bfloat16)


def combine(ids, own, up, down, twin, cross_up, cross_down, before, chunk, chunks):
    tokens, columns = twin.shape
    flat = [own, up, down, twin, cross_up, cross_down]
    specs = [
        pl.BlockSpec((None, tokens, columns), lambda g, ids: (0, 0, 0))
        if a.ndim == 3
        else pl.BlockSpec((tokens, columns), lambda g, ids: (0, 0))
        for a in flat
    ]
    args = flat
    aliases = {}
    if before is not None:
        specs = specs + [pl.BlockSpec(memory_space=pl.ANY)]
        args = flat + [before]
        aliases = {7: 0}
    return pl.pallas_call(
        combine_kernel,
        out_shape=jax.ShapeDtypeStruct((2 * tokens, columns * chunks), jnp.bfloat16),
        grid_spec=pltpu.PrefetchScalarGridSpec(
            num_scalar_prefetch=1,
            grid=(1,),
            in_specs=specs,
            out_specs=pl.BlockSpec((2 * tokens, columns), lambda g, ids: (0, chunk)),
        ),
        input_output_aliases=aliases,
        name="combine",
    )(ids, *args)


swap = [(0, 1), (1, 0)]


def add_rounded(*values):
    total = values[0].astype(jnp.float32)
    for value in values[1:]:
        total = total + value.astype(jnp.float32)
    return total.astype(jnp.bfloat16)


def line_reduce(partial):
    count = len(partial)
    up = down = None
    for t in range(1, count):
        send_up = partial[t] if up is None else add_rounded(partial[t], up)
        send_down = partial[count - t] if down is None else add_rounded(partial[count - t], down)
        ups = [(z, z + 1) for z in range(t)]
        downs = [(count - 1 - z, count - 2 - z) for z in range(t)]
        if t + 1 < count:
            up = lax.ppermute(send_up, "section", ups)
            down = lax.ppermute(send_down, "section", downs)
    crossed = lambda pairs: [(2 * i + c, 2 * j + 1 - c) for i, j in pairs for c in range(2)]
    twin = lax.ppermute(partial[0][1], "ctx", swap)
    return (
        partial[0],
        lax.ppermute(send_up[0], "section", ups),
        lax.ppermute(send_down[0], "section", downs),
        twin,
        lax.ppermute(send_up[1], ("section", "ctx"), crossed(ups)),
        lax.ppermute(send_down[1], ("section", "ctx"), crossed(downs)),
    )


def on_device(queries, slice_kv, cache_keys, cache_values, block_table, slice_index, out_weight):
    slice_len, heads, head_dim = queries.shape
    section_count = lax.axis_size("section")
    ctx_count = lax.axis_size("ctx")
    head_count = lax.axis_size("head")
    group_count = lax.axis_size("group")
    section = lax.axis_index("section")
    ctx = lax.axis_index("ctx")
    head = lax.axis_index("head")
    group = lax.axis_index("group")
    ids = jnp.stack([section, ctx, head, group]).astype(jnp.int32)
    tokens = slice_len // ctx_count
    block_len = cache_keys.shape[2]
    piece = head_dim // section_count
    width = out_weight.shape[2]
    w_local = out_weight.reshape(heads * piece, width)
    out_columns = width // head_count
    pairs = (
        head_count == 2
        and group_count == 2
        and piece % 16 == 0
        and heads % 2 == 0
        and out_columns % (128 * column_chunks) == 0
    )

    keys_far = lax.ppermute(cache_keys[0], "ctx", swap)
    values_far = lax.ppermute(cache_values[0], "ctx", swap)
    own_queries = lax.dynamic_slice_in_dim(queries, ctx * tokens, tokens, 0)
    q = jnp.swapaxes(own_queries, 0, 1)
    own = jnp.swapaxes(slice_kv, 0, 1)
    blocks = [own, cache_keys[0], cache_values[0], keys_far, values_far]
    if pairs:
        parts = 2
        columns = out_columns // column_chunks
        half_rows = w_local.shape[0] // 2
        w_one, w_two, twin_one, twin_two = ([None] * column_chunks for _ in range(4))
        for chunk in range(column_chunks):
            sent = lax.dynamic_slice(
                w_local,
                (group * half_rows, (1 - head) * out_columns + chunk * columns),
                (half_rows, columns),
            )
            w_one[chunk] = lax.ppermute(sent, "head", swap)
        twin_local = lax.ppermute(w_local, "ctx", swap)
        near = [[None] * parts for _ in range(section_count)]
        far = [[None] * parts for _ in range(section_count)]
        arrays = blocks
        for i in range(parts):
            made, packed = attend(
                ids, block_table, slice_index, q, arrays, block_len, i * (heads // parts),
                heads // parts, section_count, i == 0,
            )
            if i == 0:
                arrays = packed
            near[0][i] = made[0]
            for k in shift_order(section_count):
                near[k][i] = lax.ppermute(
                    made[k],
                    "section",
                    [(z, (z + k) % section_count) for z in range(section_count)],
                )
            for k in sum(shift_sets(section_count), []):
                far[k][i] = lax.ppermute(near[k][i], "head", swap)
        for chunk in range(column_chunks):
            w_two[chunk] = lax.ppermute(w_one[chunk], "group", swap)
            twin_one[chunk] = lax.ppermute(w_one[chunk], "ctx", swap)
            twin_two[chunk] = lax.ppermute(w_two[chunk], "ctx", swap)
        partial = [[None] * section_count for _ in range(column_chunks)]
        for shifts in shift_sets(section_count):
            for chunk in range(column_chunks):
                weights = [w_local, w_one[chunk], w_two[chunk], twin_local, twin_one[chunk], twin_two[chunk]]
                made = project(
                    ids, [near[k] for k in shifts], [far[k] for k in shifts], weights, chunk, columns
                )
                for k, value in zip(shifts, made):
                    partial[chunk][k] = value
        out = None
        for chunk in range(column_chunks):
            out = combine(ids, *line_reduce(partial[chunk]), out, chunk, column_chunks)
        return out

    attended = attend(ids, block_table, slice_index, q, blocks, block_len, 0, heads, 1, True)[0][0]
    by_section = attended.reshape(section_count, piece, heads, tokens).transpose(0, 3, 2, 1)
    by_section = by_section.reshape(section_count, tokens, heads * piece)
    by_section = lax.all_gather(by_section, "ctx", axis=1, tiled=True)
    rows = lax.all_to_all(by_section, "section", 0, 0)
    rows = rows.reshape(section_count * slice_len, heads * piece)
    rows = lax.all_gather(rows, "head", axis=1, tiled=True)
    weights = lax.all_to_all(w_local, "head", split_axis=1, concat_axis=0, tiled=True)
    partial = jnp.dot(rows, weights, preferred_element_type=jnp.float32).astype(jnp.bfloat16)
    return lax.psum_scatter(partial, "section", scatter_dimension=0, tiled=True)


def shift_order(sections):
    return sorted(range(1, sections), key=lambda k: min(k, sections - k))


def shift_sets(sections):
    first = sorted({1, sections - 1})
    return [first, [k for k in range(1, sections) if k not in first] + [0]]


def solution(mesh):
    placed = (
        P(("group", "section"), "head", None),
        P(("group", "section"), None, None),
        P(("group", "section"), "ctx", None, None),
        P(("group", "section"), "ctx", None, None),
        P("group", None),
        P("group"),
        P("head", "section", "ctx"),
    )

    return jax.shard_map(
        on_device,
        mesh=mesh,
        in_specs=placed,
        out_specs=P(("group", "section"), ("ctx", "head")),
        check_vma=False,
    )
```

```python
import functools
import math

import jax
import jax.numpy as jnp
from jax import lax
from jax.experimental import pallas as pl
from jax.experimental.pallas import tpu as pltpu
from jax.sharding import PartitionSpec as P


BPS = 4

negative_floor = -1e30
chunk_parts = (3, 3, 3, 3)


def attend_kernel(ids_ref, table_ref, index_ref, q_ref, *refs, first, pieces, block_len):
    if first:
        own_ref, kl_ref, vl_ref, kr_ref, vr_ref = refs[:5]
        out_refs = refs[5:-4]
        k_s, vt_s, m_s, acc_s = refs[-4:]
    else:
        k_s, vt_s = refs[:2]
        out_refs = refs[2:-2]
        m_s, acc_s = refs[-2:]
    heads, tokens, head_dim = q_ref.shape
    pool = table_ref.shape[1]
    section = ids_ref[0]
    ctx = ids_ref[1]
    slice_len = k_s.shape[0] - pool * block_len
    steps = index_ref[section] + 1
    width = BPS * block_len
    factor = math.log2(math.e) / math.sqrt(head_dim)

    if first:
        local_pool = kl_ref.shape[0]
        k_s[:slice_len, :] = own_ref[0]
        vt_s[:head_dim, :slice_len] = own_ref[1].T
        vt_s[head_dim:, :] = jnp.ones((vt_s.shape[0] - head_dim, vt_s.shape[1]), vt_s.dtype)

        @pl.loop(0, steps * BPS)
        def _(j):
            place = lax.rem(table_ref[section, j] + pool - ctx * local_pool, pool)
            rows = pl.ds(pl.multiple_of(slice_len + j * block_len, block_len), block_len)

            @pl.when(place < local_pool)
            def _():
                k_s[rows, :] = kl_ref[place]
                vt_s[:head_dim, rows] = vl_ref[place].T

            @pl.when(place >= local_pool)
            def _():
                k_s[rows, :] = kr_ref[place - local_pool]
                vt_s[:head_dim, rows] = vr_ref[place - local_pool].T

    q = q_ref[...].reshape(heads * tokens, head_dim)

    def scores(keys):
        return lax.dot_general(
            keys, q, (((1,), (1,)), ((), ())), preferred_element_type=jnp.float32
        )

    shape = (slice_len, heads * tokens)
    token = lax.rem(lax.broadcasted_iota(jnp.int32, shape, 1), tokens) + ctx * tokens
    s = jnp.where(
        lax.broadcasted_iota(jnp.int32, shape, 0) <= token, scores(k_s[:slice_len, :]), negative_floor
    )
    m = jnp.max(s, axis=0, keepdims=True)
    p = jnp.exp2(s * factor - m * factor).astype(jnp.bfloat16)
    m_s[...] = jnp.broadcast_to(m, m_s.shape)
    acc_s[...] = jnp.dot(vt_s[:, :slice_len], p, preferred_element_type=jnp.float32)

    @pl.loop(0, steps)
    def _(j):
        rows = pl.ds(pl.multiple_of(slice_len + j * width, block_len), width)
        s = scores(k_s[rows, :])
        before = m_s[:1, :]
        m = jnp.maximum(before, jnp.max(s, axis=0, keepdims=True))
        p = jnp.exp2(s * factor - m * factor).astype(jnp.bfloat16)
        rescale = jnp.exp2((before - m) * factor)
        m_s[...] = jnp.broadcast_to(m, m_s.shape)
        acc_s[...] = acc_s[...] * rescale + jnp.dot(
            vt_s[:, rows], p, preferred_element_type=jnp.float32
        )

    acc_s[:head_dim, :] = acc_s[:head_dim, :] / acc_s[head_dim : head_dim + 1, :]
    if pieces == 1:
        out_refs[0][...] = acc_s[:head_dim, :].astype(jnp.bfloat16)
    else:
        piece = head_dim // pieces
        for k in range(pieces):
            rows = pl.ds(pl.multiple_of(lax.bitwise_xor(section, k) * piece, piece), piece)
            for h in range(heads):
                out_refs[k // 2][k % 2, h * piece : (h + 1) * piece, :] = acc_s[
                    rows, h * tokens : (h + 1) * tokens
                ].astype(jnp.bfloat16)


def attend(ids, block_table, slice_index, q, arrays, block_len, first_head, heads, pieces, first):
    tokens, head_dim = q.shape[1:]
    whole = lambda a: pl.BlockSpec(a.shape, lambda g, *_: (0,) * a.ndim)
    pool = block_table.shape[1]
    if first:
        keys = arrays[0].shape[1] + pool * arrays[1].shape[1]
        packed = [
            jax.ShapeDtypeStruct((keys, head_dim), jnp.bfloat16),
            jax.ShapeDtypeStruct((head_dim + 16, keys), jnp.bfloat16),
        ]
    else:
        packed = []
    if pieces == 1:
        out_shape = [jax.ShapeDtypeStruct((head_dim, heads * tokens), jnp.bfloat16)]
    else:
        out_shape = [
            jax.ShapeDtypeStruct((2, heads * head_dim // pieces, tokens), jnp.bfloat16)
        ] * (pieces // 2)
    block = first_head // heads
    outs = pl.pallas_call(
        functools.partial(attend_kernel, first=first, pieces=pieces, block_len=block_len),
        out_shape=out_shape + packed,
        grid_spec=pltpu.PrefetchScalarGridSpec(
            num_scalar_prefetch=3,
            grid=(1,),
            in_specs=[pl.BlockSpec((heads, tokens, head_dim), lambda g, *_: (block, 0, 0))]
            + [whole(a) for a in arrays],
            out_specs=[whole(a) for a in out_shape + packed],
            scratch_shapes=[
                pltpu.VMEM((8, heads * tokens), jnp.float32),
                pltpu.VMEM((head_dim + 16, heads * tokens), jnp.float32),
            ],
        ),
        compiler_params=pltpu.CompilerParams(dimension_semantics=("arbitrary",)),
        name="attend",
    )(ids, block_table, slice_index, q, *arrays)
    return list(outs[: len(out_shape)]), list(outs[len(out_shape) :])


def project_kernel(ids_ref, *refs, parts):
    a_refs = refs[: 4 * parts]
    w_refs = refs[4 * parts : 4 * parts + 4]
    w_pairs = refs[4 * parts + 2 : 4 * parts + 4]
    kept, sent, a_s, w_s = refs[4 * parts + 4 :]
    rows, tokens = a_refs[0].shape[1:]
    columns = kept.shape[2]
    ctx, head, group = ids_ref[1], ids_ref[2], ids_ref[3]
    local_rows = parts * rows
    for i in range(parts):
        place = local_rows + lax.rem(i + group, parts) * rows
        place = pl.ds(pl.multiple_of(place, rows), rows)
        for which in range(4):
            core = ctx if which % 2 == 0 else 1 - ctx
            at = pl.multiple_of((which // 2 * 2 + core) * tokens, tokens)
            at = pl.ds(at, tokens)
            a_s[at, i * rows : (i + 1) * rows] = a_refs[4 * i + which][0].T
            a_s[at, place] = a_refs[4 * i + which][1].T
    for side in range(2):
        at = slice(side * columns, (side + 1) * columns)
        w_s[:local_rows, at] = w_refs[side][...]
        half = head if side == 0 else 1 - head
        for j in range(2):
            w_s[local_rows + j * rows : local_rows + (j + 1) * rows, at] = w_pairs[j][half]
    out = jnp.dot(a_s[...], w_s[...], preferred_element_type=jnp.float32).astype(jnp.bfloat16)
    for k in range(2):
        at = slice(2 * k * tokens, 2 * (k + 1) * tokens)
        sent[k] = out[at, columns:]
        kept[k] = out[at, :columns]


def project(ids, pieces, w_local, w_pairs, base, columns):
    parts = len(pieces)
    rows, tokens = pieces[0][0].shape[1:]
    flat = [a for four in pieces for a in four]
    half = w_local.shape[1] // 2
    whole = lambda a: pl.BlockSpec(a.shape, lambda n, ids: (0,) * a.ndim)
    element = lambda f: pl.BlockSpec(
        (pl.Element(w_local.shape[0]), pl.Element(columns)), lambda n, ids: (0, f(ids))
    )
    shape = jax.ShapeDtypeStruct((2, 2 * tokens, columns), jnp.bfloat16)
    return pl.pallas_call(
        functools.partial(project_kernel, parts=parts),
        out_shape=[shape, shape],
        grid_spec=pltpu.PrefetchScalarGridSpec(
            num_scalar_prefetch=1,
            grid=(1,),
            in_specs=[whole(a) for a in flat]
            + [
                element(lambda ids: pl.multiple_of(ids[2] * half + base, 128)),
                element(lambda ids: pl.multiple_of((1 - ids[2]) * half + base, 128)),
            ]
            + [whole(w) for w in w_pairs],
            out_specs=[whole(shape), whole(shape)],
            scratch_shapes=[
                pltpu.VMEM((4 * tokens, 2 * parts * rows), jnp.bfloat16),
                pltpu.VMEM((2 * parts * rows, 2 * columns), jnp.bfloat16),
            ],
        ),
        compiler_params=pltpu.CompilerParams(dimension_semantics=("arbitrary",)),
        name="project",
    )(ids, *flat, w_local, w_local, *w_pairs)


swap = [(0, 1), (1, 0)]


def add_rounded(*values):
    total = values[0].astype(jnp.float32)
    for value in values[1:]:
        total = total + value.astype(jnp.float32)
    return total.astype(jnp.bfloat16)


def on_device(queries, slice_kv, cache_keys, cache_values, block_table, slice_index, out_weight):
    slice_len, heads, head_dim = queries.shape
    section_count = lax.axis_size("section")
    ctx_count = lax.axis_size("ctx")
    head_count = lax.axis_size("head")
    group_count = lax.axis_size("group")
    section = lax.axis_index("section")
    ctx = lax.axis_index("ctx")
    head = lax.axis_index("head")
    group = lax.axis_index("group")
    ids = jnp.stack([section, ctx, head, group]).astype(jnp.int32)
    tokens = slice_len // ctx_count
    block_len = cache_keys.shape[2]
    piece = head_dim // section_count
    width = out_weight.shape[2]
    w_local = out_weight.reshape(heads * piece, width)
    out_columns = width // head_count
    pairs = fits_pairs(head_count, group_count, section_count) and (
        piece % 16 == 0 and heads % 2 == 0 and out_columns % (128 * sum(chunk_parts)) == 0
    )

    keys_far = lax.ppermute(cache_keys[0], "ctx", swap)
    values_far = lax.ppermute(cache_values[0], "ctx", swap)
    own_queries = lax.dynamic_slice_in_dim(queries, ctx * tokens, tokens, 0)
    q = jnp.swapaxes(own_queries, 0, 1)
    own = jnp.swapaxes(slice_kv, 0, 1)
    blocks = [own, cache_keys[0], cache_values[0], keys_far, values_far]
    if pairs:
        parts = 2
        pair = [(z, z ^ 1) for z in range(section_count)]
        across = [(z, z ^ 2) for z in range(section_count)]
        widths = [out_columns * w // sum(chunk_parts) for w in chunk_parts]
        bases = [sum(widths[:j]) for j in range(len(widths))]
        half_rows = w_local.shape[0] // 2
        w_pairs = []
        for base, columns in zip(bases, widths):
            cut = lambda at: lax.dynamic_slice(w_local, (group * half_rows, at), (half_rows, columns))
            sent = jnp.stack([cut(base), cut(out_columns + base)])
            through_pair = lax.ppermute(sent, "section", pair)
            w_pairs.append((through_pair, lax.ppermute(through_pair, "group", swap)))
        arrays = blocks
        pieces = []
        for i in range(parts):
            (kept, sent), packed = attend(
                ids, block_table, slice_index, q, arrays, block_len, i * (heads // parts),
                heads // parts, section_count, i == 0,
            )
            if i == 0:
                arrays = packed
            far = lax.ppermute(sent, "section", across)
            kept_twin = lax.ppermute(kept, "ctx", swap)
            far_twin = lax.ppermute(far, "ctx", swap)
            pieces.append((kept, kept_twin, far, far_twin))
        out = []
        for j, (base, columns) in enumerate(zip(bases, widths)):
            kept, sent = project(ids, pieces, w_local, w_pairs[j], base, columns)
            other = lax.ppermute(sent, "head", swap)
            far = lax.ppermute(add_rounded(kept[1], other[1]), "section", across)
            out.append(add_rounded(kept[0], other[0], far))
        return jnp.concatenate(out, axis=1)

    attended = attend(ids, block_table, slice_index, q, blocks, block_len, 0, heads, 1, True)[0][0]
    by_section = attended.reshape(section_count, piece, heads, tokens).transpose(0, 3, 2, 1)
    by_section = by_section.reshape(section_count, tokens, heads * piece)
    by_section = lax.all_gather(by_section, "ctx", axis=1, tiled=True)
    rows = lax.all_to_all(by_section, "section", 0, 0)
    rows = rows.reshape(section_count * slice_len, heads * piece)
    rows = lax.all_gather(rows, "head", axis=1, tiled=True)
    weights = lax.all_to_all(w_local, "head", split_axis=1, concat_axis=0, tiled=True)
    partial = jnp.dot(rows, weights, preferred_element_type=jnp.float32).astype(jnp.bfloat16)
    return lax.psum_scatter(partial, "section", scatter_dimension=0, tiled=True)


def fits_pairs(head_count, group_count, section_count):
    return head_count == 2 and group_count == 2 and section_count == 4


def solution(mesh):
    placed = (
        P(("group", "section"), "head", None),
        P(("group", "section"), None, None),
        P(("group", "section"), "ctx", None, None),
        P(("group", "section"), "ctx", None, None),
        P("group", None),
        P("group"),
        P("head", "section", "ctx"),
    )

    return jax.shard_map(
        on_device,
        mesh=mesh,
        in_specs=placed,
        out_specs=P(("group", "section"), ("ctx", "head")),
        check_vma=False,
    )
```

```python
import functools
import math

import jax
import jax.numpy as jnp
from jax import lax
from jax.experimental import pallas as pl
from jax.experimental.pallas import tpu as pltpu
from jax.sharding import PartitionSpec as P


BPS = 4

negative_floor = -1e30
chunk_parts = (3, 3, 3, 3)


def attend_kernel(ids_ref, table_ref, index_ref, q_ref, *refs, first, pieces, block_len):
    if first:
        own_ref, kl_ref, vl_ref, kr_ref, vr_ref = refs[:5]
        out_refs = refs[5:-4]
        k_s, vt_s, m_s, acc_s = refs[-4:]
    else:
        k_s, vt_s = refs[:2]
        out_refs = refs[2:-2]
        m_s, acc_s = refs[-2:]
    heads, tokens, head_dim = q_ref.shape
    pool = table_ref.shape[1]
    section = ids_ref[0]
    ctx = ids_ref[1]
    slice_len = k_s.shape[0] - pool * block_len
    steps = index_ref[section] + 1
    width = BPS * block_len
    factor = math.log2(math.e) / math.sqrt(head_dim)

    if first:
        local_pool = kl_ref.shape[0]
        k_s[:slice_len, :] = own_ref[:, 0, :]
        vt_s[:head_dim, :slice_len] = own_ref[:, 1, :].T
        vt_s[head_dim:, :] = jnp.ones((vt_s.shape[0] - head_dim, vt_s.shape[1]), vt_s.dtype)

        @pl.loop(0, steps * BPS)
        def _(j):
            place = lax.rem(table_ref[section, j] + pool - ctx * local_pool, pool)
            rows = pl.ds(pl.multiple_of(slice_len + j * block_len, block_len), block_len)

            @pl.when(place < local_pool)
            def _():
                k_s[rows, :] = kl_ref[place]
                vt_s[:head_dim, rows] = vl_ref[place].T

            @pl.when(place >= local_pool)
            def _():
                k_s[rows, :] = kr_ref[place - local_pool]
                vt_s[:head_dim, rows] = vr_ref[place - local_pool].T

    q = q_ref[...].reshape(heads * tokens, head_dim)

    def scores(keys):
        return lax.dot_general(
            keys, q, (((1,), (1,)), ((), ())), preferred_element_type=jnp.float32
        )

    shape = (slice_len, heads * tokens)
    token = lax.rem(lax.broadcasted_iota(jnp.int32, shape, 1), tokens) + ctx * tokens
    s = jnp.where(
        lax.broadcasted_iota(jnp.int32, shape, 0) <= token, scores(k_s[:slice_len, :]), negative_floor
    )
    m = jnp.max(s, axis=0, keepdims=True)
    p = jnp.exp2(s * factor - m * factor).astype(jnp.bfloat16)
    m_s[...] = jnp.broadcast_to(m, m_s.shape)
    acc_s[...] = jnp.dot(vt_s[:, :slice_len], p, preferred_element_type=jnp.float32)

    @pl.loop(0, steps)
    def _(j):
        rows = pl.ds(pl.multiple_of(slice_len + j * width, block_len), width)
        s = scores(k_s[rows, :])
        before = m_s[:1, :]
        m = jnp.maximum(before, jnp.max(s, axis=0, keepdims=True))
        p = jnp.exp2(s * factor - m * factor).astype(jnp.bfloat16)
        rescale = jnp.exp2((before - m) * factor)
        m_s[...] = jnp.broadcast_to(m, m_s.shape)
        acc_s[...] = acc_s[...] * rescale + jnp.dot(
            vt_s[:, rows], p, preferred_element_type=jnp.float32
        )

    acc_s[:head_dim, :] = acc_s[:head_dim, :] / acc_s[head_dim : head_dim + 1, :]
    if pieces == 1:
        out_refs[0][...] = acc_s[:head_dim, :].astype(jnp.bfloat16)
    else:
        piece = head_dim // pieces
        for k in range(pieces):
            rows = pl.ds(pl.multiple_of(lax.bitwise_xor(section, k) * piece, piece), piece)
            for h in range(heads):
                out_refs[k // 2][k % 2, h * piece : (h + 1) * piece, :] = acc_s[
                    rows, h * tokens : (h + 1) * tokens
                ].astype(jnp.bfloat16)


def attend(ids, block_table, slice_index, q, arrays, block_len, first_head, heads, pieces, first):
    tokens, head_dim = q.shape[1:]
    whole = lambda a: pl.BlockSpec(a.shape, lambda g, *_: (0,) * a.ndim)
    pool = block_table.shape[1]
    if first:
        keys = arrays[0].shape[0] + pool * arrays[1].shape[1]
        packed = [
            jax.ShapeDtypeStruct((keys, head_dim), jnp.bfloat16),
            jax.ShapeDtypeStruct((head_dim + 16, keys), jnp.bfloat16),
        ]
    else:
        packed = []
    if pieces == 1:
        out_shape = [jax.ShapeDtypeStruct((head_dim, heads * tokens), jnp.bfloat16)]
    else:
        out_shape = [
            jax.ShapeDtypeStruct((2, heads * head_dim // pieces, tokens), jnp.bfloat16)
        ] * (pieces // 2)
    block = first_head // heads
    outs = pl.pallas_call(
        functools.partial(attend_kernel, first=first, pieces=pieces, block_len=block_len),
        out_shape=out_shape + packed,
        grid_spec=pltpu.PrefetchScalarGridSpec(
            num_scalar_prefetch=3,
            grid=(1,),
            in_specs=[pl.BlockSpec((heads, tokens, head_dim), lambda g, *_: (block, 0, 0))]
            + [whole(a) for a in arrays],
            out_specs=[whole(a) for a in out_shape + packed],
            scratch_shapes=[
                pltpu.VMEM((8, heads * tokens), jnp.float32),
                pltpu.VMEM((head_dim + 16, heads * tokens), jnp.float32),
            ],
        ),
        compiler_params=pltpu.CompilerParams(dimension_semantics=("arbitrary",)),
        name="attend",
    )(ids, block_table, slice_index, q, *arrays)
    return list(outs[: len(out_shape)]), list(outs[len(out_shape) :])


def cut_kernel(ids_ref, w_ref, out_ref):
    out_ref[0] = w_ref[...]


def cut(ids, w_local, base, columns):
    rows = w_local.shape[0] // 2
    half = w_local.shape[1] // 2
    return pl.pallas_call(
        cut_kernel,
        out_shape=jax.ShapeDtypeStruct((2, rows, columns), jnp.bfloat16),
        grid_spec=pltpu.PrefetchScalarGridSpec(
            num_scalar_prefetch=1,
            grid=(2,),
            in_specs=[
                pl.BlockSpec(
                    (pl.Element(rows), pl.Element(columns)),
                    lambda n, ids: (
                        pl.multiple_of(ids[3] * rows, 16),
                        pl.multiple_of(n * half + base, 128),
                    ),
                )
            ],
            out_specs=pl.BlockSpec((1, rows, columns), lambda n, ids: (n, 0, 0)),
        ),
        name="cut",
    )(ids, w_local)


def project_kernel(ids_ref, *refs, inputs, first):
    w_refs = refs[inputs : inputs + 2]
    w_pairs = refs[inputs + 2 : inputs + 4]
    kept, sent = refs[inputs + 4 : inputs + 6]
    w_s = refs[-1]
    half = kept.shape[1]
    ctx, head, group = ids_ref[1], ids_ref[2], ids_ref[3]
    local_rows = w_refs[0].shape[0]
    if first:
        a_s = refs[inputs + 6]
        parts = inputs // 4
        rows, tokens = refs[0].shape[1:]
        for i in range(parts):
            place = local_rows + lax.rem(i + group, parts) * rows
            place = pl.ds(pl.multiple_of(place, rows), rows)
            for which in range(4):
                core = ctx if which % 2 == 0 else 1 - ctx
                at = pl.multiple_of((which // 2 * 2 + core) * tokens, tokens)
                at = pl.ds(at, tokens)
                a_s[at, i * rows : (i + 1) * rows] = refs[4 * i + which][0].T
                a_s[at, place] = refs[4 * i + which][1].T
    else:
        a_s = refs[0]
    pair_rows = w_pairs[0].shape[1]
    for side, out_ref in ((1, sent), (0, kept)):
        which = head if side == 0 else 1 - head
        for j in range(2):
            w_s[j * pair_rows : (j + 1) * pair_rows, :] = w_pairs[j][which]
        out = jnp.dot(
            a_s[:, :local_rows], w_refs[side][...], preferred_element_type=jnp.float32
        ) + jnp.dot(a_s[:, local_rows:], w_s[...], preferred_element_type=jnp.float32)
        for k in range(2):
            out_ref[k] = out[k * half : (k + 1) * half].astype(jnp.bfloat16)


def project(ids, flat, w_local, w_pairs, base, columns, first):
    half = w_local.shape[1] // 2
    whole = lambda a: pl.BlockSpec(a.shape, lambda n, ids: (0,) * a.ndim)
    element = lambda f: pl.BlockSpec(
        (pl.Element(w_local.shape[0]), pl.Element(columns)), lambda n, ids: (0, f(ids))
    )
    if first:
        rows = 4 * flat[0].shape[2]
        depth = w_local.shape[0] + 2 * w_pairs[0].shape[1]
        made = [jax.ShapeDtypeStruct((rows, depth), jnp.bfloat16)]
    else:
        rows = flat[0].shape[0]
        made = []
    shape = jax.ShapeDtypeStruct((2, rows // 2, columns), jnp.bfloat16)
    return pl.pallas_call(
        functools.partial(project_kernel, inputs=len(flat), first=first),
        out_shape=[shape, shape] + made,
        grid_spec=pltpu.PrefetchScalarGridSpec(
            num_scalar_prefetch=1,
            grid=(1,),
            in_specs=[whole(a) for a in flat]
            + [
                element(lambda ids: pl.multiple_of(ids[2] * half + base, 128)),
                element(lambda ids: pl.multiple_of((1 - ids[2]) * half + base, 128)),
            ]
            + [whole(w) for w in w_pairs],
            out_specs=[whole(a) for a in [shape, shape] + made],
            scratch_shapes=[pltpu.VMEM((2 * w_pairs[0].shape[1], columns), jnp.bfloat16)],
        ),
        compiler_params=pltpu.CompilerParams(dimension_semantics=("arbitrary",)),
        name="project",
    )(ids, *flat, w_local, w_local, *w_pairs)


swap = [(0, 1), (1, 0)]


def add_rounded(*values):
    total = values[0].astype(jnp.float32)
    for value in values[1:]:
        total = total + value.astype(jnp.float32)
    return total.astype(jnp.bfloat16)


def on_device(queries, slice_kv, cache_keys, cache_values, block_table, slice_index, out_weight):
    slice_len, heads, head_dim = queries.shape
    section_count = lax.axis_size("section")
    ctx_count = lax.axis_size("ctx")
    head_count = lax.axis_size("head")
    group_count = lax.axis_size("group")
    section = lax.axis_index("section")
    ctx = lax.axis_index("ctx")
    head = lax.axis_index("head")
    group = lax.axis_index("group")
    ids = jnp.stack([section, ctx, head, group]).astype(jnp.int32)
    tokens = slice_len // ctx_count
    block_len = cache_keys.shape[2]
    piece = head_dim // section_count
    width = out_weight.shape[2]
    w_local = out_weight.reshape(heads * piece, width)
    out_columns = width // head_count
    pairs = fits_pairs(head_count, group_count, section_count) and (
        piece % 16 == 0 and heads % 2 == 0 and out_columns % (128 * sum(chunk_parts)) == 0
    )

    keys_far = lax.ppermute(cache_keys[0], "ctx", swap)
    values_far = lax.ppermute(cache_values[0], "ctx", swap)
    own_queries = lax.dynamic_slice_in_dim(queries, ctx * tokens, tokens, 0)
    q = jnp.swapaxes(own_queries, 0, 1)
    blocks = [slice_kv, cache_keys[0], cache_values[0], keys_far, values_far]
    if pairs:
        parts = 2
        pair = [(z, z ^ 1) for z in range(section_count)]
        across = [(z, z ^ 2) for z in range(section_count)]
        widths = [out_columns * w // sum(chunk_parts) for w in chunk_parts]
        bases = [sum(widths[:j]) for j in range(len(widths))]
        w_pairs = []
        for base, columns in zip(bases, widths):
            sent = cut(ids, w_local, base, columns)
            through_pair = lax.ppermute(sent, "section", pair)
            w_pairs.append((through_pair, lax.ppermute(through_pair, "group", swap)))
        arrays = blocks
        pieces = []
        for i in range(parts):
            (kept, sent), packed = attend(
                ids, block_table, slice_index, q, arrays, block_len, i * (heads // parts),
                heads // parts, section_count, i == 0,
            )
            if i == 0:
                arrays = packed
            far = lax.ppermute(sent, "section", across)
            kept_twin = lax.ppermute(kept, "ctx", swap)
            far_twin = lax.ppermute(far, "ctx", swap)
            pieces += [kept, kept_twin, far, far_twin]
        out = []
        for j, (base, columns) in enumerate(zip(bases, widths)):
            kept, sent, *made = project(ids, pieces, w_local, w_pairs[j], base, columns, j == 0)
            pieces = made or pieces
            other = lax.ppermute(sent, "head", swap)
            far = lax.ppermute(add_rounded(kept[1], other[1]), "section", across)
            out.append(add_rounded(kept[0], other[0], far))
        return jnp.concatenate(out, axis=1)

    attended = attend(ids, block_table, slice_index, q, blocks, block_len, 0, heads, 1, True)[0][0]
    by_section = attended.reshape(section_count, piece, heads, tokens).transpose(0, 3, 2, 1)
    by_section = by_section.reshape(section_count, tokens, heads * piece)
    by_section = lax.all_gather(by_section, "ctx", axis=1, tiled=True)
    rows = lax.all_to_all(by_section, "section", 0, 0)
    rows = rows.reshape(section_count * slice_len, heads * piece)
    rows = lax.all_gather(rows, "head", axis=1, tiled=True)
    weights = lax.all_to_all(w_local, "head", split_axis=1, concat_axis=0, tiled=True)
    partial = jnp.dot(rows, weights, preferred_element_type=jnp.float32).astype(jnp.bfloat16)
    return lax.psum_scatter(partial, "section", scatter_dimension=0, tiled=True)


def fits_pairs(head_count, group_count, section_count):
    return head_count == 2 and group_count == 2 and section_count == 4


def solution(mesh):
    placed = (
        P(("group", "section"), "head", None),
        P(("group", "section"), None, None),
        P(("group", "section"), "ctx", None, None),
        P(("group", "section"), "ctx", None, None),
        P("group", None),
        P("group"),
        P("head", "section", "ctx"),
    )

    return jax.shard_map(
        on_device,
        mesh=mesh,
        in_specs=placed,
        out_specs=P(("group", "section"), ("ctx", "head")),
        check_vma=False,
    )
```

```python
import functools
import math

import jax
import jax.numpy as jnp
from jax import lax
from jax.experimental import pallas as pl
from jax.experimental.pallas import tpu as pltpu
from jax.sharding import PartitionSpec as P


BPS = 4

negative_floor = -1e30
chunk_parts = (3, 4, 3, 2)


def attend_kernel(ids_ref, table_ref, index_ref, q_ref, *refs, first, pieces, block_len):
    if first:
        own_ref, kl_ref, vl_ref, kr_ref, vr_ref = refs[:5]
        out_refs = refs[5:-4]
        k_s, vt_s, m_s, acc_s = refs[-4:]
    else:
        k_s, vt_s = refs[:2]
        out_refs = refs[2:-2]
        m_s, acc_s = refs[-2:]
    heads, tokens, head_dim = q_ref.shape
    pool = table_ref.shape[1]
    section = ids_ref[0]
    ctx = ids_ref[1]
    slice_len = k_s.shape[0] - pool * block_len
    steps = index_ref[section] + 1
    width = BPS * block_len
    factor = math.log2(math.e) / math.sqrt(head_dim)

    if first:
        local_pool = kl_ref.shape[0]
        k_s[:slice_len, :] = own_ref[:, 0, :]
        vt_s[:head_dim, :slice_len] = own_ref[:, 1, :].T
        vt_s[head_dim:, :] = jnp.ones((vt_s.shape[0] - head_dim, vt_s.shape[1]), vt_s.dtype)

        @pl.loop(0, steps * BPS)
        def _(j):
            place = lax.rem(table_ref[section, j] + pool - ctx * local_pool, pool)
            rows = pl.ds(pl.multiple_of(slice_len + j * block_len, block_len), block_len)

            @pl.when(place < local_pool)
            def _():
                k_s[rows, :] = kl_ref[place]
                vt_s[:head_dim, rows] = vl_ref[place].T

            @pl.when(place >= local_pool)
            def _():
                k_s[rows, :] = kr_ref[place - local_pool]
                vt_s[:head_dim, rows] = vr_ref[place - local_pool].T

    q = q_ref[...].reshape(heads * tokens, head_dim)

    def scores(keys):
        return lax.dot_general(
            keys, q, (((1,), (1,)), ((), ())), preferred_element_type=jnp.float32
        )

    shape = (slice_len, heads * tokens)
    token = lax.rem(lax.broadcasted_iota(jnp.int32, shape, 1), tokens) + ctx * tokens
    s = jnp.where(
        lax.broadcasted_iota(jnp.int32, shape, 0) <= token, scores(k_s[:slice_len, :]), negative_floor
    )
    m = jnp.max(s, axis=0, keepdims=True)
    p = jnp.exp2(s * factor - m * factor).astype(jnp.bfloat16)
    m_s[...] = jnp.broadcast_to(m, m_s.shape)
    acc_s[...] = jnp.dot(vt_s[:, :slice_len], p, preferred_element_type=jnp.float32)

    @pl.loop(0, steps)
    def _(j):
        rows = pl.ds(pl.multiple_of(slice_len + j * width, block_len), width)
        s = scores(k_s[rows, :])
        before = m_s[:1, :]
        m = jnp.maximum(before, jnp.max(s, axis=0, keepdims=True))
        p = jnp.exp2(s * factor - m * factor).astype(jnp.bfloat16)
        rescale = jnp.exp2((before - m) * factor)
        m_s[...] = jnp.broadcast_to(m, m_s.shape)
        acc_s[...] = acc_s[...] * rescale + jnp.dot(
            vt_s[:, rows], p, preferred_element_type=jnp.float32
        )

    acc_s[:head_dim, :] = acc_s[:head_dim, :] / acc_s[head_dim : head_dim + 1, :]
    if pieces == 1:
        out_refs[0][...] = acc_s[:head_dim, :].astype(jnp.bfloat16)
    else:
        piece = head_dim // pieces
        for k in range(pieces):
            rows = pl.ds(pl.multiple_of(lax.bitwise_xor(section, k) * piece, piece), piece)
            for h in range(heads):
                out_refs[k // 2][k % 2, h * piece : (h + 1) * piece, :] = acc_s[
                    rows, h * tokens : (h + 1) * tokens
                ].astype(jnp.bfloat16)


def attend(ids, block_table, slice_index, q, arrays, block_len, first_head, heads, pieces, first):
    tokens, head_dim = q.shape[1:]
    whole = lambda a: pl.BlockSpec(a.shape, lambda g, *_: (0,) * a.ndim)
    pool = block_table.shape[1]
    if first:
        keys = arrays[0].shape[0] + pool * arrays[1].shape[1]
        packed = [
            jax.ShapeDtypeStruct((keys, head_dim), jnp.bfloat16),
            jax.ShapeDtypeStruct((head_dim + 16, keys), jnp.bfloat16),
        ]
    else:
        packed = []
    if pieces == 1:
        out_shape = [jax.ShapeDtypeStruct((head_dim, heads * tokens), jnp.bfloat16)]
    else:
        out_shape = [
            jax.ShapeDtypeStruct((2, heads * head_dim // pieces, tokens), jnp.bfloat16)
        ] * (pieces // 2)
    block = first_head // heads
    outs = pl.pallas_call(
        functools.partial(attend_kernel, first=first, pieces=pieces, block_len=block_len),
        out_shape=out_shape + packed,
        grid_spec=pltpu.PrefetchScalarGridSpec(
            num_scalar_prefetch=3,
            grid=(1,),
            in_specs=[pl.BlockSpec((heads, tokens, head_dim), lambda g, *_: (block, 0, 0))]
            + [whole(a) for a in arrays],
            out_specs=[whole(a) for a in out_shape + packed],
            scratch_shapes=[
                pltpu.VMEM((8, heads * tokens), jnp.float32),
                pltpu.VMEM((head_dim + 16, heads * tokens), jnp.float32),
            ],
        ),
        compiler_params=pltpu.CompilerParams(dimension_semantics=("arbitrary",)),
        name="attend",
    )(ids, block_table, slice_index, q, *arrays)
    return list(outs[: len(out_shape)]), list(outs[len(out_shape) :])


def cut_kernel(ids_ref, w_ref, out_ref, sems, *, base):
    rows, columns = out_ref.shape[1:]
    at = pl.ds(pl.multiple_of(ids_ref[3] * rows, rows), rows)
    half = w_ref.shape[1] // 2
    copies = [
        pltpu.make_async_copy(
            w_ref.at[at, pl.ds(n * half + base, columns)], out_ref.at[n], sems.at[n]
        )
        for n in range(2)
    ]
    for copy in copies:
        copy.start()
    for copy in copies:
        copy.wait()


def cut(ids, w_local, base, columns):
    rows = w_local.shape[0] // 2
    return pl.pallas_call(
        functools.partial(cut_kernel, base=base),
        out_shape=jax.ShapeDtypeStruct((2, rows, columns), jnp.bfloat16),
        grid_spec=pltpu.PrefetchScalarGridSpec(
            num_scalar_prefetch=1,
            grid=(1,),
            in_specs=[pl.BlockSpec(memory_space=pl.ANY)],
            out_specs=pl.BlockSpec((2, rows, columns), lambda n, ids: (0, 0, 0)),
            scratch_shapes=[pltpu.SemaphoreType.DMA((2,))],
        ),
        name="cut",
    )(ids, w_local)


def project_kernel(ids_ref, *refs, inputs, first):
    w_refs = refs[inputs : inputs + 2]
    w_pairs = refs[inputs + 2 : inputs + 4]
    kept, sent = refs[inputs + 4 : inputs + 6]
    w_s = refs[-1]
    half = kept.shape[1]
    ctx, head, group = ids_ref[1], ids_ref[2], ids_ref[3]
    local_rows = w_refs[0].shape[0]
    if first:
        a_s = refs[inputs + 6]
        parts = inputs // 4
        rows, tokens = refs[0].shape[1:]
        for i in range(parts):
            place = local_rows + lax.rem(i + group, parts) * rows
            place = pl.ds(pl.multiple_of(place, rows), rows)
            for which in range(4):
                core = ctx if which % 2 == 0 else 1 - ctx
                at = pl.multiple_of((which // 2 * 2 + core) * tokens, tokens)
                at = pl.ds(at, tokens)
                a_s[at, i * rows : (i + 1) * rows] = refs[4 * i + which][0].T
                a_s[at, place] = refs[4 * i + which][1].T
    else:
        a_s = refs[0]
    pair_rows = w_pairs[0].shape[1]
    for side, out_ref in ((1, sent), (0, kept)):
        which = head if side == 0 else 1 - head
        for j in range(2):
            w_s[j * pair_rows : (j + 1) * pair_rows, :] = w_pairs[j][which]
        out = jnp.dot(
            a_s[:, :local_rows], w_refs[side][...], preferred_element_type=jnp.float32
        ) + jnp.dot(a_s[:, local_rows:], w_s[...], preferred_element_type=jnp.float32)
        for k in range(2):
            out_ref[k] = out[k * half : (k + 1) * half].astype(jnp.bfloat16)


def project(ids, flat, w_local, w_pairs, base, columns, first):
    half = w_local.shape[1] // 2
    whole = lambda a: pl.BlockSpec(a.shape, lambda n, ids: (0,) * a.ndim)
    element = lambda f: pl.BlockSpec(
        (pl.Element(w_local.shape[0]), pl.Element(columns)), lambda n, ids: (0, f(ids))
    )
    if first:
        rows = 4 * flat[0].shape[2]
        depth = w_local.shape[0] + 2 * w_pairs[0].shape[1]
        made = [jax.ShapeDtypeStruct((rows, depth), jnp.bfloat16)]
    else:
        rows = flat[0].shape[0]
        made = []
    shape = jax.ShapeDtypeStruct((2, rows // 2, columns), jnp.bfloat16)
    return pl.pallas_call(
        functools.partial(project_kernel, inputs=len(flat), first=first),
        out_shape=[shape, shape] + made,
        grid_spec=pltpu.PrefetchScalarGridSpec(
            num_scalar_prefetch=1,
            grid=(1,),
            in_specs=[whole(a) for a in flat]
            + [
                element(lambda ids: pl.multiple_of(ids[2] * half + base, 128)),
                element(lambda ids: pl.multiple_of((1 - ids[2]) * half + base, 128)),
            ]
            + [whole(w) for w in w_pairs],
            out_specs=[whole(a) for a in [shape, shape] + made],
            scratch_shapes=[pltpu.VMEM((2 * w_pairs[0].shape[1], columns), jnp.bfloat16)],
        ),
        compiler_params=pltpu.CompilerParams(dimension_semantics=("arbitrary",)),
        name="project",
    )(ids, *flat, w_local, w_local, *w_pairs)


swap = [(0, 1), (1, 0)]


def add_rounded(*values):
    total = values[0].astype(jnp.float32)
    for value in values[1:]:
        total = total + value.astype(jnp.float32)
    return total.astype(jnp.bfloat16)


def on_device(queries, slice_kv, cache_keys, cache_values, block_table, slice_index, out_weight):
    slice_len, heads, head_dim = queries.shape
    section_count = lax.axis_size("section")
    ctx_count = lax.axis_size("ctx")
    head_count = lax.axis_size("head")
    group_count = lax.axis_size("group")
    section = lax.axis_index("section")
    ctx = lax.axis_index("ctx")
    head = lax.axis_index("head")
    group = lax.axis_index("group")
    ids = jnp.stack([section, ctx, head, group]).astype(jnp.int32)
    tokens = slice_len // ctx_count
    block_len = cache_keys.shape[2]
    piece = head_dim // section_count
    width = out_weight.shape[2]
    w_local = out_weight.reshape(heads * piece, width)
    out_columns = width // head_count
    pairs = fits_pairs(head_count, group_count, section_count) and (
        piece % 16 == 0 and heads % 2 == 0 and out_columns % (128 * sum(chunk_parts)) == 0
    )

    keys_far = lax.ppermute(cache_keys[0], "ctx", swap)
    values_far = lax.ppermute(cache_values[0], "ctx", swap)
    own_queries = lax.dynamic_slice_in_dim(queries, ctx * tokens, tokens, 0)
    q = jnp.swapaxes(own_queries, 0, 1)
    blocks = [slice_kv, cache_keys[0], cache_values[0], keys_far, values_far]
    if pairs:
        parts = 2
        pair = [(z, z ^ 1) for z in range(section_count)]
        across = [(z, z ^ 2) for z in range(section_count)]
        widths = [out_columns * w // sum(chunk_parts) for w in chunk_parts]
        bases = [sum(widths[:j]) for j in range(len(widths))]
        w_pairs = []
        for base, columns in zip(bases, widths):
            sent = cut(ids, w_local, base, columns)
            through_pair = lax.ppermute(sent, "section", pair)
            w_pairs.append((through_pair, lax.ppermute(through_pair, "group", swap)))
        arrays = blocks
        pieces = []
        for i in range(parts):
            (kept, sent), packed = attend(
                ids, block_table, slice_index, q, arrays, block_len, i * (heads // parts),
                heads // parts, section_count, i == 0,
            )
            if i == 0:
                arrays = packed
            far = lax.ppermute(sent, "section", across)
            kept_twin = lax.ppermute(kept, "ctx", swap)
            far_twin = lax.ppermute(far, "ctx", swap)
            pieces += [kept, kept_twin, far, far_twin]
        out = []
        for j, (base, columns) in enumerate(zip(bases, widths)):
            kept, sent, *made = project(ids, pieces, w_local, w_pairs[j], base, columns, j == 0)
            pieces = made or pieces
            other = lax.ppermute(sent, "head", swap)
            far = lax.ppermute(add_rounded(kept[1], other[1]), "section", across)
            out.append(add_rounded(kept[0], other[0], far))
        return jnp.concatenate(out, axis=1)

    attended = attend(ids, block_table, slice_index, q, blocks, block_len, 0, heads, 1, True)[0][0]
    by_section = attended.reshape(section_count, piece, heads, tokens).transpose(0, 3, 2, 1)
    by_section = by_section.reshape(section_count, tokens, heads * piece)
    by_section = lax.all_gather(by_section, "ctx", axis=1, tiled=True)
    rows = lax.all_to_all(by_section, "section", 0, 0)
    rows = rows.reshape(section_count * slice_len, heads * piece)
    rows = lax.all_gather(rows, "head", axis=1, tiled=True)
    weights = lax.all_to_all(w_local, "head", split_axis=1, concat_axis=0, tiled=True)
    partial = jnp.dot(rows, weights, preferred_element_type=jnp.float32).astype(jnp.bfloat16)
    return lax.psum_scatter(partial, "section", scatter_dimension=0, tiled=True)


def fits_pairs(head_count, group_count, section_count):
    return head_count == 2 and group_count == 2 and section_count == 4


def solution(mesh):
    placed = (
        P(("group", "section"), "head", None),
        P(("group", "section"), None, None),
        P(("group", "section"), "ctx", None, None),
        P(("group", "section"), "ctx", None, None),
        P("group", None),
        P("group"),
        P("head", "section", "ctx"),
    )

    return jax.shard_map(
        on_device,
        mesh=mesh,
        in_specs=placed,
        out_specs=P(("group", "section"), ("ctx", "head")),
        check_vma=False,
    )
```

```python
import functools
import math

import jax
import jax.numpy as jnp
from jax import lax
from jax.experimental import pallas as pl
from jax.experimental.pallas import tpu as pltpu
from jax.sharding import PartitionSpec as P


BPS = 4

negative_floor = -1e30
chunk_parts = (3, 4, 3, 2)


def attend_kernel(ids_ref, table_ref, index_ref, q_ref, *refs, first, pieces, block_len):
    if first:
        own_ref, kl_ref, vl_ref, kr_ref, vr_ref = refs[:5]
        out_refs = refs[5:-4]
        k_s, vt_s, m_s, acc_s = refs[-4:]
    else:
        k_s, vt_s = refs[:2]
        out_refs = refs[2:-2]
        m_s, acc_s = refs[-2:]
    heads, tokens, head_dim = q_ref.shape
    pool = table_ref.shape[1]
    section = ids_ref[0]
    ctx = ids_ref[1]
    slice_len = k_s.shape[0] - pool * block_len
    steps = index_ref[section] + 1
    width = BPS * block_len
    factor = math.log2(math.e) / math.sqrt(head_dim)

    if first:
        local_pool = kl_ref.shape[0]
        k_s[:slice_len, :] = own_ref[:, 0, :]
        vt_s[:head_dim, :slice_len] = own_ref[:, 1, :].T
        vt_s[head_dim:, :] = jnp.ones((vt_s.shape[0] - head_dim, vt_s.shape[1]), vt_s.dtype)

        @pl.loop(0, steps * BPS)
        def _(j):
            place = lax.rem(table_ref[section, j] + pool - ctx * local_pool, pool)
            rows = pl.ds(pl.multiple_of(slice_len + j * block_len, block_len), block_len)

            @pl.when(place < local_pool)
            def _():
                k_s[rows, :] = kl_ref[place]
                vt_s[:head_dim, rows] = vl_ref[place].T

            @pl.when(place >= local_pool)
            def _():
                k_s[rows, :] = kr_ref[place - local_pool]
                vt_s[:head_dim, rows] = vr_ref[place - local_pool].T

    q = q_ref[...].reshape(heads * tokens, head_dim)

    def scores(keys):
        return lax.dot_general(
            keys, q, (((1,), (1,)), ((), ())), preferred_element_type=jnp.float32
        )

    shape = (slice_len, heads * tokens)
    token = lax.rem(lax.broadcasted_iota(jnp.int32, shape, 1), tokens) + ctx * tokens
    s = jnp.where(
        lax.broadcasted_iota(jnp.int32, shape, 0) <= token, scores(k_s[:slice_len, :]), negative_floor
    )
    m = jnp.max(s, axis=0, keepdims=True)
    p = jnp.exp2(s * factor - m * factor).astype(jnp.bfloat16)
    m_s[...] = jnp.broadcast_to(m, m_s.shape)
    acc_s[...] = jnp.dot(vt_s[:, :slice_len], p, preferred_element_type=jnp.float32)

    @pl.loop(0, steps)
    def _(j):
        rows = pl.ds(pl.multiple_of(slice_len + j * width, block_len), width)
        s = scores(k_s[rows, :])
        before = m_s[:1, :]
        m = jnp.maximum(before, jnp.max(s, axis=0, keepdims=True))
        p = jnp.exp2(s * factor - m * factor).astype(jnp.bfloat16)
        rescale = jnp.exp2((before - m) * factor)
        m_s[...] = jnp.broadcast_to(m, m_s.shape)
        acc_s[...] = acc_s[...] * rescale + jnp.dot(
            vt_s[:, rows], p, preferred_element_type=jnp.float32
        )

    acc_s[:head_dim, :] = acc_s[:head_dim, :] / acc_s[head_dim : head_dim + 1, :]
    if pieces == 1:
        out_refs[0][...] = acc_s[:head_dim, :].astype(jnp.bfloat16)
    else:
        piece = head_dim // pieces
        for k in range(pieces):
            rows = pl.ds(pl.multiple_of(lax.bitwise_xor(section, k) * piece, piece), piece)
            for h in range(heads):
                out_refs[k // 2][k % 2, h * piece : (h + 1) * piece, :] = acc_s[
                    rows, h * tokens : (h + 1) * tokens
                ].astype(jnp.bfloat16)


def attend(ids, block_table, slice_index, q, arrays, block_len, first_head, heads, pieces, first):
    tokens, head_dim = q.shape[1:]
    whole = lambda a: pl.BlockSpec(a.shape, lambda g, *_: (0,) * a.ndim)
    pool = block_table.shape[1]
    if first:
        keys = arrays[0].shape[0] + pool * arrays[1].shape[1]
        packed = [
            jax.ShapeDtypeStruct((keys, head_dim), jnp.bfloat16),
            jax.ShapeDtypeStruct((head_dim + 16, keys), jnp.bfloat16),
        ]
    else:
        packed = []
    if pieces == 1:
        out_shape = [jax.ShapeDtypeStruct((head_dim, heads * tokens), jnp.bfloat16)]
    else:
        out_shape = [
            jax.ShapeDtypeStruct((2, heads * head_dim // pieces, tokens), jnp.bfloat16)
        ] * (pieces // 2)
    block = first_head // heads
    outs = pl.pallas_call(
        functools.partial(attend_kernel, first=first, pieces=pieces, block_len=block_len),
        out_shape=out_shape + packed,
        grid_spec=pltpu.PrefetchScalarGridSpec(
            num_scalar_prefetch=3,
            grid=(1,),
            in_specs=[pl.BlockSpec((heads, tokens, head_dim), lambda g, *_: (block, 0, 0))]
            + [whole(a) for a in arrays],
            out_specs=[whole(a) for a in out_shape + packed],
            scratch_shapes=[
                pltpu.VMEM((8, heads * tokens), jnp.float32),
                pltpu.VMEM((head_dim + 16, heads * tokens), jnp.float32),
            ],
        ),
        compiler_params=pltpu.CompilerParams(dimension_semantics=("arbitrary",)),
        name="attend",
    )(ids, block_table, slice_index, q, *arrays)
    return list(outs[: len(out_shape)]), list(outs[len(out_shape) :])


def project_kernel(ids_ref, *refs, inputs, first):
    w_refs = refs[inputs : inputs + 2]
    w_pairs = refs[inputs + 2 : inputs + 4]
    kept, sent = refs[inputs + 4 : inputs + 6]
    w_s = refs[-1]
    half = kept.shape[1]
    ctx, head, group = ids_ref[1], ids_ref[2], ids_ref[3]
    local_rows = w_refs[0].shape[0]
    if first:
        a_s = refs[inputs + 6]
        parts = inputs // 4
        rows, tokens = refs[0].shape[1:]
        for i in range(parts):
            place = local_rows + lax.rem(i + group, parts) * rows
            place = pl.ds(pl.multiple_of(place, rows), rows)
            for which in range(4):
                core = ctx if which % 2 == 0 else 1 - ctx
                at = pl.multiple_of((which // 2 * 2 + core) * tokens, tokens)
                at = pl.ds(at, tokens)
                a_s[at, i * rows : (i + 1) * rows] = refs[4 * i + which][0].T
                a_s[at, place] = refs[4 * i + which][1].T
    else:
        a_s = refs[0]
    pair_rows = w_pairs[0].shape[1]
    for side, out_ref in ((1, sent), (0, kept)):
        which = head if side == 0 else 1 - head
        for j in range(2):
            w_s[j * pair_rows : (j + 1) * pair_rows, :] = w_pairs[j][which]
        out = jnp.dot(
            a_s[:, :local_rows], w_refs[side][...], preferred_element_type=jnp.float32
        ) + jnp.dot(a_s[:, local_rows:], w_s[...], preferred_element_type=jnp.float32)
        for k in range(2):
            out_ref[k] = out[k * half : (k + 1) * half].astype(jnp.bfloat16)


def project(ids, flat, w_local, w_pairs, base, columns, first):
    half = w_local.shape[1] // 2
    whole = lambda a: pl.BlockSpec(a.shape, lambda n, ids: (0,) * a.ndim)
    element = lambda f: pl.BlockSpec(
        (pl.Element(w_local.shape[0]), pl.Element(columns)), lambda n, ids: (0, f(ids))
    )
    if first:
        rows = 4 * flat[0].shape[2]
        depth = w_local.shape[0] + 2 * w_pairs[0].shape[1]
        made = [jax.ShapeDtypeStruct((rows, depth), jnp.bfloat16)]
    else:
        rows = flat[0].shape[0]
        made = []
    shape = jax.ShapeDtypeStruct((2, rows // 2, columns), jnp.bfloat16)
    return pl.pallas_call(
        functools.partial(project_kernel, inputs=len(flat), first=first),
        out_shape=[shape, shape] + made,
        grid_spec=pltpu.PrefetchScalarGridSpec(
            num_scalar_prefetch=1,
            grid=(1,),
            in_specs=[whole(a) for a in flat]
            + [
                element(lambda ids: pl.multiple_of(ids[2] * half + base, 128)),
                element(lambda ids: pl.multiple_of((1 - ids[2]) * half + base, 128)),
            ]
            + [whole(w) for w in w_pairs],
            out_specs=[whole(a) for a in [shape, shape] + made],
            scratch_shapes=[pltpu.VMEM((2 * w_pairs[0].shape[1], columns), jnp.bfloat16)],
        ),
        compiler_params=pltpu.CompilerParams(dimension_semantics=("arbitrary",)),
        name="project",
    )(ids, *flat, w_local, w_local, *w_pairs)


swap = [(0, 1), (1, 0)]


def add_rounded(*values):
    total = values[0].astype(jnp.float32)
    for value in values[1:]:
        total = total + value.astype(jnp.float32)
    return total.astype(jnp.bfloat16)


def on_device(queries, slice_kv, cache_keys, cache_values, block_table, slice_index, out_weight):
    slice_len, heads, head_dim = queries.shape
    section_count = lax.axis_size("section")
    ctx_count = lax.axis_size("ctx")
    head_count = lax.axis_size("head")
    group_count = lax.axis_size("group")
    section = lax.axis_index("section")
    ctx = lax.axis_index("ctx")
    head = lax.axis_index("head")
    group = lax.axis_index("group")
    ids = jnp.stack([section, ctx, head, group]).astype(jnp.int32)
    tokens = slice_len // ctx_count
    block_len = cache_keys.shape[2]
    piece = head_dim // section_count
    width = out_weight.shape[2]
    w_local = out_weight.reshape(heads * piece, width)
    out_columns = width // head_count
    pairs = fits_pairs(head_count, group_count, section_count) and (
        piece % 16 == 0 and heads % 2 == 0 and out_columns % (128 * sum(chunk_parts)) == 0
    )

    keys_far = lax.ppermute(cache_keys[0], "ctx", swap)
    values_far = lax.ppermute(cache_values[0], "ctx", swap)
    own_queries = lax.dynamic_slice_in_dim(queries, ctx * tokens, tokens, 0)
    q = jnp.swapaxes(own_queries, 0, 1)
    blocks = [slice_kv, cache_keys[0], cache_values[0], keys_far, values_far]
    if pairs:
        parts = 2
        pair = [(z, z ^ 1) for z in range(section_count)]
        across = [(z, z ^ 2) for z in range(section_count)]
        widths = [out_columns * w // sum(chunk_parts) for w in chunk_parts]
        bases = [sum(widths[:j]) for j in range(len(widths))]
        half_rows = w_local.shape[0] // 2
        w_pairs = []
        for base, columns in zip(bases, widths):
            cut = lambda at: lax.dynamic_slice(w_local, (group * half_rows, at), (half_rows, columns))
            sent = jnp.stack([cut(base), cut(out_columns + base)])
            through_pair = lax.ppermute(sent, "section", pair)
            w_pairs.append((through_pair, lax.ppermute(through_pair, "group", swap)))
        arrays = blocks
        pieces = []
        for i in range(parts):
            (kept, sent), packed = attend(
                ids, block_table, slice_index, q, arrays, block_len, i * (heads // parts),
                heads // parts, section_count, i == 0,
            )
            if i == 0:
                arrays = packed
            far = lax.ppermute(sent, "section", across)
            kept_twin = lax.ppermute(kept, "ctx", swap)
            far_twin = lax.ppermute(far, "ctx", swap)
            pieces += [kept, kept_twin, far, far_twin]
        out = []
        for j, (base, columns) in enumerate(zip(bases, widths)):
            kept, sent, *made = project(ids, pieces, w_local, w_pairs[j], base, columns, j == 0)
            pieces = made or pieces
            other = lax.ppermute(sent, "head", swap)
            far = lax.ppermute(add_rounded(kept[1], other[1]), "section", across)
            out.append(add_rounded(kept[0], other[0], far))
        return jnp.concatenate(out, axis=1)

    attended = attend(ids, block_table, slice_index, q, blocks, block_len, 0, heads, 1, True)[0][0]
    by_section = attended.reshape(section_count, piece, heads, tokens).transpose(0, 3, 2, 1)
    by_section = by_section.reshape(section_count, tokens, heads * piece)
    by_section = lax.all_gather(by_section, "ctx", axis=1, tiled=True)
    rows = lax.all_to_all(by_section, "section", 0, 0)
    rows = rows.reshape(section_count * slice_len, heads * piece)
    rows = lax.all_gather(rows, "head", axis=1, tiled=True)
    weights = lax.all_to_all(w_local, "head", split_axis=1, concat_axis=0, tiled=True)
    partial = jnp.dot(rows, weights, preferred_element_type=jnp.float32).astype(jnp.bfloat16)
    return lax.psum_scatter(partial, "section", scatter_dimension=0, tiled=True)


def fits_pairs(head_count, group_count, section_count):
    return head_count == 2 and group_count == 2 and section_count == 4


def solution(mesh):
    placed = (
        P(("group", "section"), "head", None),
        P(("group", "section"), None, None),
        P(("group", "section"), "ctx", None, None),
        P(("group", "section"), "ctx", None, None),
        P("group", None),
        P("group"),
        P("head", "section", "ctx"),
    )

    return jax.shard_map(
        on_device,
        mesh=mesh,
        in_specs=placed,
        out_specs=P(("group", "section"), ("ctx", "head")),
        check_vma=False,
    )
```

```python
import functools
import math

import jax
import jax.numpy as jnp
from jax import lax
from jax.experimental import pallas as pl
from jax.experimental.pallas import tpu as pltpu
from jax.sharding import PartitionSpec as P


BPS = 4

negative_floor = -1e30
chunk_parts = ((3,), (4,), (3,), (2,))
head_parts = (2, 4)


def attend_kernel(ids_ref, table_ref, index_ref, q_ref, *refs, first, pieces, block_len):
    if first:
        own_ref, kl_ref, vl_ref, kr_ref, vr_ref = refs[:5]
        out_refs = refs[5:-4]
        k_s, vt_s, m_s, acc_s = refs[-4:]
    else:
        k_s, vt_s = refs[:2]
        out_refs = refs[2:-2]
        m_s, acc_s = refs[-2:]
    heads, tokens, head_dim = q_ref.shape
    pool = table_ref.shape[1]
    section = ids_ref[0]
    ctx = ids_ref[1]
    slice_len = k_s.shape[0] - pool * block_len
    steps = index_ref[section] + 1
    width = BPS * block_len
    factor = math.log2(math.e) / math.sqrt(head_dim)

    if first:
        local_pool = kl_ref.shape[0]
        k_s[:slice_len, :] = own_ref[:, 0, :]
        vt_s[:head_dim, :slice_len] = own_ref[:, 1, :].T
        vt_s[head_dim:, :] = jnp.ones((vt_s.shape[0] - head_dim, vt_s.shape[1]), vt_s.dtype)

        @pl.loop(0, steps * BPS)
        def _(j):
            place = lax.rem(table_ref[section, j] + pool - ctx * local_pool, pool)
            rows = pl.ds(pl.multiple_of(slice_len + j * block_len, block_len), block_len)

            @pl.when(place < local_pool)
            def _():
                k_s[rows, :] = kl_ref[place]
                vt_s[:head_dim, rows] = vl_ref[place].T

            @pl.when(place >= local_pool)
            def _():
                k_s[rows, :] = kr_ref[place - local_pool]
                vt_s[:head_dim, rows] = vr_ref[place - local_pool].T

    q = q_ref[...].reshape(heads * tokens, head_dim)

    def scores(keys):
        return lax.dot_general(
            keys, q, (((1,), (1,)), ((), ())), preferred_element_type=jnp.float32
        )

    shape = (slice_len, heads * tokens)
    token = lax.rem(lax.broadcasted_iota(jnp.int32, shape, 1), tokens) + ctx * tokens
    s = jnp.where(
        lax.broadcasted_iota(jnp.int32, shape, 0) <= token, scores(k_s[:slice_len, :]), negative_floor
    )
    m = jnp.max(s, axis=0, keepdims=True)
    p = jnp.exp2(s * factor - m * factor).astype(jnp.bfloat16)
    m_s[...] = jnp.broadcast_to(m, m_s.shape)
    acc_s[...] = jnp.dot(vt_s[:, :slice_len], p, preferred_element_type=jnp.float32)

    @pl.loop(0, steps)
    def _(j):
        rows = pl.ds(pl.multiple_of(slice_len + j * width, block_len), width)
        s = scores(k_s[rows, :])
        before = m_s[:1, :]
        m = jnp.maximum(before, jnp.max(s, axis=0, keepdims=True))
        p = jnp.exp2(s * factor - m * factor).astype(jnp.bfloat16)
        rescale = jnp.exp2((before - m) * factor)
        m_s[...] = jnp.broadcast_to(m, m_s.shape)
        acc_s[...] = acc_s[...] * rescale + jnp.dot(
            vt_s[:, rows], p, preferred_element_type=jnp.float32
        )

    inverse = 1.0 / acc_s[head_dim : head_dim + 1, :]
    acc_s[:head_dim, :] = acc_s[:head_dim, :] * inverse
    if pieces == 1:
        out_refs[0][...] = acc_s[:head_dim, :].astype(jnp.bfloat16)
    else:
        piece = head_dim // pieces
        for k in range(pieces):
            rows = pl.ds(pl.multiple_of(lax.bitwise_xor(section, k) * piece, piece), piece)
            for h in range(heads):
                out_refs[k // 2][k % 2, h * piece : (h + 1) * piece, :] = acc_s[
                    rows, h * tokens : (h + 1) * tokens
                ].astype(jnp.bfloat16)


def attend(ids, block_table, slice_index, q, arrays, block_len, first_head, heads, pieces, first):
    tokens, head_dim = q.shape[1:]
    whole = lambda a: pl.BlockSpec(a.shape, lambda g, *_: (0,) * a.ndim)
    pool = block_table.shape[1]
    if first:
        keys = arrays[0].shape[0] + pool * arrays[1].shape[1]
        packed = [
            jax.ShapeDtypeStruct((keys, head_dim), jnp.bfloat16),
            jax.ShapeDtypeStruct((head_dim + 16, keys), jnp.bfloat16),
        ]
    else:
        packed = []
    if pieces == 1:
        out_shape = [jax.ShapeDtypeStruct((head_dim, heads * tokens), jnp.bfloat16)]
    else:
        out_shape = [
            jax.ShapeDtypeStruct((2, heads * head_dim // pieces, tokens), jnp.bfloat16)
        ] * (pieces // 2)
    outs = pl.pallas_call(
        functools.partial(attend_kernel, first=first, pieces=pieces, block_len=block_len),
        out_shape=out_shape + packed,
        grid_spec=pltpu.PrefetchScalarGridSpec(
            num_scalar_prefetch=3,
            grid=(1,),
            in_specs=[
                pl.BlockSpec(
                    (pl.Element(heads), pl.Element(tokens), pl.Element(head_dim)),
                    lambda g, *_: (first_head, 0, 0),
                )
            ]
            + [whole(a) for a in arrays],
            out_specs=[whole(a) for a in out_shape + packed],
            scratch_shapes=[
                pltpu.VMEM((8, heads * tokens), jnp.float32),
                pltpu.VMEM((head_dim + 16, heads * tokens), jnp.float32),
            ],
        ),
        compiler_params=pltpu.CompilerParams(dimension_semantics=("arbitrary",)),
        name="attend",
    )(ids, block_table, slice_index, q, *arrays)
    return list(outs[: len(out_shape)]), list(outs[len(out_shape) :])


def project_kernel(ids_ref, *refs, inputs, first):
    w_refs = refs[inputs : inputs + 2]
    made = 3 if first else 2
    w_pairs = refs[inputs + 2 : -1 - made]
    kept, sent = refs[-1 - made : 1 - made]
    w_s = refs[-1]
    half = kept.shape[1]
    ctx, head, group = ids_ref[1], ids_ref[2], ids_ref[3]
    local_rows = w_refs[0].shape[0]
    if first:
        a_s = refs[-2]
        half_rows = local_rows // 2
        tokens = refs[0].shape[2]
        base = 0
        for i in range(0, inputs, 4):
            rows = refs[i].shape[1]
            cuts = sorted({0, rows, min(max(half_rows - base, 0), rows)})
            for which in range(4):
                core = ctx if which % 2 == 0 else 1 - ctx
                at = pl.multiple_of((which // 2 * 2 + core) * tokens, tokens)
                at = pl.ds(at, tokens)
                a_s[at, base : base + rows] = refs[i + which][0].T
                for start, stop in zip(cuts, cuts[1:]):
                    side, inside = divmod(base + start, half_rows)
                    place = local_rows + lax.rem(side + group, 2) * half_rows + inside
                    place = pl.ds(pl.multiple_of(place, 128), stop - start)
                    a_s[at, place] = refs[i + which][1, start:stop].T
            base += rows
    else:
        a_s = refs[0]
    pair_rows = w_pairs[0].shape[1]
    for side, out_ref in ((1, sent), (0, kept)):
        which = head if side == 0 else 1 - head
        start = 0
        for i, w_ref in enumerate(w_pairs):
            at = (i % 2) * pair_rows
            part = w_ref.shape[2]
            w_s[at : at + pair_rows, start : start + part] = w_ref[which]
            start += part * (i % 2)
        out = jnp.dot(
            a_s[:, :local_rows], w_refs[side][...], preferred_element_type=jnp.float32
        ) + jnp.dot(a_s[:, local_rows:], w_s[...], preferred_element_type=jnp.float32)
        for k in range(2):
            out_ref[k] = out[k * half : (k + 1) * half].astype(jnp.bfloat16)


def project(ids, flat, w_local, w_pairs, base, columns, first):
    half = w_local.shape[1] // 2
    whole = lambda a: pl.BlockSpec(a.shape, lambda n, ids: (0,) * a.ndim)
    element = lambda f: pl.BlockSpec(
        (pl.Element(w_local.shape[0]), pl.Element(columns)), lambda n, ids: (0, f(ids))
    )
    if first:
        rows = 4 * flat[0].shape[2]
        depth = w_local.shape[0] + 2 * w_pairs[0].shape[1]
        made = [jax.ShapeDtypeStruct((rows, depth), jnp.bfloat16)]
    else:
        rows = flat[0].shape[0]
        made = []
    shape = jax.ShapeDtypeStruct((2, rows // 2, columns), jnp.bfloat16)
    return pl.pallas_call(
        functools.partial(project_kernel, inputs=len(flat), first=first),
        out_shape=[shape, shape] + made,
        grid_spec=pltpu.PrefetchScalarGridSpec(
            num_scalar_prefetch=1,
            grid=(1,),
            in_specs=[whole(a) for a in flat]
            + [
                element(lambda ids: pl.multiple_of(ids[2] * half + base, 128)),
                element(lambda ids: pl.multiple_of((1 - ids[2]) * half + base, 128)),
            ]
            + [whole(w) for w in w_pairs],
            out_specs=[whole(a) for a in [shape, shape] + made],
            scratch_shapes=[pltpu.VMEM((2 * w_pairs[0].shape[1], columns), jnp.bfloat16)],
        ),
        compiler_params=pltpu.CompilerParams(dimension_semantics=("arbitrary",)),
        name="project",
    )(ids, *flat, w_local, w_local, *w_pairs)


swap = [(0, 1), (1, 0)]


def add_rounded(*values):
    total = values[0].astype(jnp.float32)
    for value in values[1:]:
        total = total + value.astype(jnp.float32)
    return total.astype(jnp.bfloat16)


def on_device(queries, slice_kv, cache_keys, cache_values, block_table, slice_index, out_weight):
    slice_len, heads, head_dim = queries.shape
    section_count = lax.axis_size("section")
    ctx_count = lax.axis_size("ctx")
    head_count = lax.axis_size("head")
    group_count = lax.axis_size("group")
    section = lax.axis_index("section")
    ctx = lax.axis_index("ctx")
    head = lax.axis_index("head")
    group = lax.axis_index("group")
    ids = jnp.stack([section, ctx, head, group]).astype(jnp.int32)
    tokens = slice_len // ctx_count
    block_len = cache_keys.shape[2]
    piece = head_dim // section_count
    width = out_weight.shape[2]
    w_local = out_weight.reshape(heads * piece, width)
    out_columns = width // head_count
    pairs = fits_pairs(head_count, group_count, section_count) and (
        piece % 16 == 0 and heads % (2 * sum(head_parts)) == 0 and out_columns % (128 * sum(map(sum, chunk_parts))) == 0
    )

    keys_far = lax.ppermute(cache_keys[0], "ctx", swap)
    values_far = lax.ppermute(cache_values[0], "ctx", swap)
    own_queries = lax.dynamic_slice_in_dim(queries, ctx * tokens, tokens, 0)
    q = jnp.swapaxes(own_queries, 0, 1)
    blocks = [slice_kv, cache_keys[0], cache_values[0], keys_far, values_far]
    if pairs:
        parts = len(head_parts)
        counts = [heads * n // sum(head_parts) for n in head_parts]
        pair = [(z, z ^ 1) for z in range(section_count)]
        across = [(z, z ^ 2) for z in range(section_count)]
        unit = out_columns // sum(map(sum, chunk_parts))
        widths = [unit * sum(parts_of) for parts_of in chunk_parts]
        bases = [sum(widths[:j]) for j in range(len(widths))]
        half_rows = w_local.shape[0] // 2

        def send_weights(w, j):
            made = []
            for i, part in enumerate(chunk_parts[j]):
                base, columns = bases[j] + unit * sum(chunk_parts[j][:i]), unit * part
                cut = lambda at: lax.dynamic_slice(w, (group * half_rows, at), (half_rows, columns))
                sent = jnp.stack([cut(base), cut(out_columns + base)])
                through_pair = lax.ppermute(sent, "section", pair)
                made += [through_pair, lax.ppermute(through_pair, "group", swap)]
            return made

        w_pairs = [send_weights(w_local, j) for j in range(2)]
        arrays = blocks
        pieces = []
        for i in range(parts):
            (kept, sent), packed = attend(
                ids, block_table, slice_index, q, arrays, block_len, sum(counts[:i]),
                counts[i], section_count, i == 0,
            )
            if i == 0:
                arrays = packed
            far = lax.ppermute(sent, "section", across)
            kept_twin = lax.ppermute(kept, "ctx", swap)
            far_twin = lax.ppermute(far, "ctx", swap)
            pieces += [kept, kept_twin, far, far_twin]
        w_late, pieces[-4] = lax.optimization_barrier((w_local, pieces[-4]))
        w_pairs += [send_weights(w_late, j) for j in range(2, len(chunk_parts))]
        out = []
        for j, (base, columns) in enumerate(zip(bases, widths)):
            kept, sent, *made = project(ids, pieces, w_local, w_pairs[j], base, columns, j == 0)
            pieces = made or pieces
            other = lax.ppermute(sent, "head", swap)
            far = lax.ppermute(add_rounded(kept[1], other[1]), "section", across)
            out.append(add_rounded(kept[0], other[0], far))
        return jnp.concatenate(out, axis=1)

    attended = attend(ids, block_table, slice_index, q, blocks, block_len, 0, heads, 1, True)[0][0]
    by_section = attended.reshape(section_count, piece, heads, tokens).transpose(0, 3, 2, 1)
    by_section = by_section.reshape(section_count, tokens, heads * piece)
    by_section = lax.all_gather(by_section, "ctx", axis=1, tiled=True)
    rows = lax.all_to_all(by_section, "section", 0, 0)
    rows = rows.reshape(section_count * slice_len, heads * piece)
    rows = lax.all_gather(rows, "head", axis=1, tiled=True)
    weights = lax.all_to_all(w_local, "head", split_axis=1, concat_axis=0, tiled=True)
    partial = jnp.dot(rows, weights, preferred_element_type=jnp.float32).astype(jnp.bfloat16)
    return lax.psum_scatter(partial, "section", scatter_dimension=0, tiled=True)


def fits_pairs(head_count, group_count, section_count):
    return head_count == 2 and group_count == 2 and section_count == 4


def solution(mesh):
    placed = (
        P(("group", "section"), "head", None),
        P(("group", "section"), None, None),
        P(("group", "section"), "ctx", None, None),
        P(("group", "section"), "ctx", None, None),
        P("group", None),
        P("group"),
        P("head", "section", "ctx"),
    )

    return jax.shard_map(
        on_device,
        mesh=mesh,
        in_specs=placed,
        out_specs=P(("group", "section"), ("ctx", "head")),
        check_vma=False,
    )
```
